32 devices in a mesh: lines: 4 (over y, x), buses: 8 (over z, core).
Axes of the slice: x: 2, y: 2, z: 4, core: 2. Of those that a mesh axis runs over, the one named last changes fastest.
Arguments:
- ptdf: bfloat16 [4096, 10240], P('lines', 'buses'), may hold values from -0.078125 to 0.078125
- load: float32 [384, 10240], P(None, 'buses'), may hold values from 0.03 to 3.8, as said below
- ratings: float32 [32768], replicated, may hold values from 0.3 to 3
- line_index: int32 [4096], P('lines'), may hold values from 0 to 32767
- gen_bus: int32 [2048], P('buses'), may hold values from 0 to 10239, as said below
- gen_quad: float32 [2048], P('buses'), may hold values from 0.05 to 0.5
- gen_lin: float32 [2048], P('buses'), may hold values from 0.5 to 2.5
- gen_max: float32 [2048], P('buses'), may hold values from 0.8 to 4
- gen_start: float32 [384, 2048], P(None, 'buses'), may hold values from 0 to 2
- stor_bus: int32 [1024], P('buses'), may hold values from 0 to 1279
- stor_quad: float32 [1024], P('buses'), may hold values from 0.05 to 0.5
- stor_rate: float32 [1024], P('buses'), may hold values from 0.3 to 1.5
- stor_energy: float32 [1024], P('buses'), may hold values from 1 to 8
- stor_start: float32 [384, 1024], P(None, 'buses'), may hold values from -0.5 to 0.5
- lam_start: float32 [384], replicated, may hold values from -4 to 4
- mu_start: float32 [384, 4096], P(None, ('lines', 'buses')), may hold values from -3 to 3
- omega_start: float32 [384, 1024], P(None, 'buses'), may hold values from -2 to 2
Outputs:
- gen_out: float32 [384, 2048], P(None, 'buses')
- stor_out: float32 [384, 1024], P(None, 'buses')
- lam_out: float32 [384], replicated
- mu_out: float32 [384, 4096], P(None, ('lines', 'buses'))
- omega_out: float32 [384, 1024], P(None, 'buses')
The draws below stay inside these ranges and needn't reach their ends.
Inputs may be any that keep to these rules, and one draw needn't show every extreme that they name: `gen_bus`: of the 256 generators of one area at most 32 sit on the buses of any one area (1280 consecutive buses); in every draw one area holds exactly 32 generators of every area, and the others of an area spread over the remaining areas as evenly as counts allow. `load`: loads are positive.
All inputs are finite; a program needn't handle non-finite values.
Results may differ from the reference program's by a relative error of at most 0.0075.
Values may be sent and summed in bfloat16 or wider, within the bound.
A program may use at most 64 MiB of HBM per device.

```python
import math
import jax
import jax.numpy as jnp

HOURS = 24
BUS_DEV = 1280
GEN_DEV = 256
STOR_DEV = 128
RATED = 32768
ROWS = 384
BUSES = 10240
LINES = 4096
GENS = 2048
STOR = 1024


def draw_load(key, part):
    area_count = BUSES // BUS_DEV
    bus_key, row_key, cell_key = jax.random.split(jax.random.fold_in(key, 11), 3)
    area_of = (jnp.arange(BUSES, dtype=jnp.int32) // BUS_DEV).astype(jnp.float32)
    rising = 1.0 + 2.0 * area_of / max(area_count - 1, 1)
    bus_factor = jax.random.uniform(bus_key, (BUSES,), jnp.float32, 0.5, 1.5)
    row_factor = jax.random.uniform(row_key, (ROWS, 1), jnp.float32, 0.7, 1.3)
    cell_factor = jax.random.uniform(cell_key, (ROWS, BUSES), jnp.float32, 0.8, 1.2)
    return (0.3 * rising[None, :] * bus_factor[None, :] * row_factor * cell_factor).astype(jnp.float32)


def draw_gen_bus(key, part):
    area_count = GENS // GEN_DEV
    slot_count = max(8, (GEN_DEV + area_count - 1) // area_count)
    hot_key, order_key, other_key, bus_key = jax.random.split(jax.random.fold_in(key, 23), 4)
    hot_area = jax.random.randint(hot_key, (), 0, area_count)
    position = jax.vmap(lambda sub_key: jax.random.permutation(sub_key, GEN_DEV))(jax.random.split(order_key, area_count))
    others = jax.vmap(lambda sub_key: jax.random.permutation(sub_key, area_count - 1))(jax.random.split(other_key, area_count))
    spill_index = jnp.maximum(position - slot_count, 0) % (area_count - 1)
    offset = jnp.take_along_axis(others, spill_index, axis=1)
    target = jnp.where(position < slot_count, hot_area, (hot_area + 1 + offset) % area_count)
    local_bus = jax.random.randint(bus_key, (area_count, GEN_DEV), 0, BUS_DEV)
    return (target * BUS_DEV + local_bus).reshape(GENS).astype(jnp.int32)


def plant(result, own_key, low, top_value):
    longest = result.shape.index(max(result.shape))
    spots = []
    for shift in (0, 1):
        where = [jax.random.randint(jax.random.fold_in(own_key, axis), (), 0, length) for axis, length in enumerate(result.shape)]
        where[longest] = (where[longest] + shift) % result.shape[longest]
        spots.append(tuple(where))
    return result.at[spots[0]].set(low).at[spots[1]].set(top_value)


def with_spikes(result, stream_key, source, target, parts, factor):
    def block_of(dim):
        return (jnp.arange(result.shape[dim]) // (result.shape[dim] // parts)).reshape((-1,) + (1,) * (result.ndim - 1 - dim))

    first = jax.random.permutation(stream_key, parts)[block_of(target)]
    other_side = (block_of(target) + parts // 2) % parts
    return jnp.where((block_of(source) == first) | (block_of(source) == other_side), factor * result, result)


def block_levels(key, shape, cuts, low, largest):
    def one(dim, parts):
        heights = jax.random.uniform(jax.random.fold_in(jax.random.fold_in(key, 6), dim), (parts,), jnp.float32, low / len(cuts), largest / len(cuts))
        return jnp.repeat(jnp.exp(heights), shape[dim] // parts).reshape((-1,) + (1,) * (len(shape) - dim - 1))

    factor_of = one(*cuts[0])
    for cut in cuts[1:]:
        factor_of = factor_of * one(*cut)
    return factor_of


def normal_values(stream_key, dims, deviation, most, shards=(), kind=jnp.bfloat16):
    factor_of = block_levels(stream_key, dims, shards, -0.22, 0.18) if shards else 1.0
    result = jax.random.normal(stream_key, dims, jnp.float32) * deviation * factor_of
    return jnp.minimum(jnp.maximum(result, -most), most).astype(kind)


def bell_draw_with(own_key, dims, spread, reach, cuts, heavy, kind=jnp.bfloat16):
    result = spread * jax.random.normal(own_key, dims, jnp.float32)
    if cuts:
        result = result * block_levels(own_key, dims, cuts, -0.22, 0.18)
    return jnp.clip(with_spikes(result, jax.random.fold_in(own_key, 3), *heavy), -reach, reach).astype(kind)


def setup_inputs(seed: int = 0) -> dict:
    splits = jax.random.split(jax.random.key(seed), 18)
    ptdf = bell_draw_with(splits[0], (LINES, BUSES), BUSES ** -0.5, 0.078125, ((0, 4), (1, 8)), (1, 0, 8, 2.0))
    load = draw_load(jax.random.fold_in(splits[17], 71), 0)
    ratings = jnp.clip(jnp.exp(jax.random.uniform(splits[2], (RATED,), jnp.float32, math.log(0.3), math.log(3.0))), 0.3, 3.0)
    line_index = plant(jax.random.randint(splits[3], (LINES,), 0, RATED), jax.random.fold_in(splits[3], 1), 0, RATED - 1).astype(jnp.int32)
    gen_bus = draw_gen_bus(jax.random.fold_in(splits[17], 71), 0)
    gen_quad = jnp.clip(jnp.exp(math.log(0.5) - 2.3025851 * jax.random.uniform(splits[5], (GENS,), jnp.float32) ** block_levels(splits[5], (GENS,), ((0, 8),), -0.2, 0.2)), 0.05, 0.5)
    gen_lin = jnp.clip(0.5 + 2.0 * jax.random.uniform(splits[6], (GENS,), jnp.float32) ** block_levels(splits[6], (GENS,), ((0, 8),), -0.2, 0.2), 0.5, 2.5)
    gen_max = jnp.clip(jnp.exp(math.log(4.0) - 1.609438 * jax.random.uniform(splits[7], (GENS,), jnp.float32) ** block_levels(splits[7], (GENS,), ((0, 8),), -0.2, 0.2)), 0.8, 4.0)
    gen_start = jnp.clip(2.0 * jax.random.uniform(splits[8], (ROWS, GENS), jnp.float32) ** block_levels(splits[8], (ROWS, GENS), ((1, 8),), -0.2, 0.2), 0.0, 2.0)
    stor_bus = plant(jax.random.randint(splits[9], (STOR,), 0, BUS_DEV), jax.random.fold_in(splits[9], 1), 0, BUS_DEV - 1).astype(jnp.int32)
    stor_quad = jnp.clip(jnp.exp(math.log(0.5) - 2.3025851 * jax.random.uniform(splits[10], (STOR,), jnp.float32) ** block_levels(splits[10], (STOR,), ((0, 8),), -0.2, 0.2)), 0.05, 0.5)
    stor_rate = jnp.clip(jnp.exp(math.log(1.5) - 1.60943787 * jax.random.uniform(splits[11], (STOR,), jnp.float32) ** block_levels(splits[11], (STOR,), ((0, 8),), -0.2, 0.2)), 0.3, 1.5)
    stor_energy = jnp.clip(jnp.exp(math.log(8.0) - 2.0794415 * jax.random.uniform(splits[12], (STOR,), jnp.float32) ** block_levels(splits[12], (STOR,), ((0, 8),), -0.2, 0.2)), 1.0, 8.0)
    stor_start = jnp.clip(jax.random.uniform(splits[13], (ROWS, STOR), jnp.float32, -0.5, 0.5) * block_levels(splits[13], (ROWS, STOR), ((1, 8),), -0.4, 0.0), -0.5, 0.5)
    lam_start = normal_values(splits[14], (ROWS,), 1.0, 4.0, (), jnp.float32)
    mu_start = normal_values(splits[15], (ROWS, LINES), 0.5, 3.0, ((1, 32),), jnp.float32)
    omega_start = normal_values(splits[16], (ROWS, STOR), 0.3, 2.0, ((1, 8),), jnp.float32)
    return dict(ptdf=ptdf, load=load, ratings=ratings, line_index=line_index, gen_bus=gen_bus, gen_quad=gen_quad, gen_lin=gen_lin, gen_max=gen_max, gen_start=gen_start, stor_bus=stor_bus, stor_quad=stor_quad, stor_rate=stor_rate, stor_energy=stor_energy, stor_start=stor_start, lam_start=lam_start, mu_start=mu_start, omega_start=omega_start)


TAU = 0.25
SIGMA_FLOW = 4.0
SIGMA_STORE = 0.25
KAPPA = 1.0
THETA = 0.5


def reverse_cum(values, hour_count):
    total_rows, columns = values.shape
    shaped = values.reshape(total_rows // hour_count, hour_count, columns)
    summed = jnp.flip(jnp.cumsum(jnp.flip(shaped, 1), axis=1), 1)
    return summed.reshape(total_rows, columns)


def forward_cum(values, hour_count):
    total_rows, columns = values.shape
    shaped = values.reshape(total_rows // hour_count, hour_count, columns)
    return jnp.cumsum(shaped, axis=1).reshape(total_rows, columns)


def dual_step(dual_now, image_term, step_size, low_bound, high_bound):
    shifted = dual_now + step_size * image_term
    return shifted - step_size * jnp.clip(shifted / step_size, low_bound, high_bound)


def reference(ptdf, load, ratings, line_index, gen_bus, gen_quad, gen_lin, gen_max, gen_start,
              stor_bus, stor_quad, stor_rate, stor_energy, stor_start, lam_start, mu_start, omega_start):
    stor_global = (jnp.arange(STOR, dtype=jnp.int32) // STOR_DEV) * BUS_DEV + stor_bus.astype(jnp.int32)
    gen_index = gen_bus.astype(jnp.int32)
    limit = jnp.take(ratings, line_index.astype(jnp.int32))
    hour_of = jnp.arange(ROWS, dtype=jnp.int32) % HOURS
    last_hour = (hour_of == HOURS - 1)[:, None]
    half_energy = (0.5 * stor_energy)[None, :]
    low_bound = jnp.where(last_hour, jnp.zeros_like(half_energy), -half_energy)
    high_bound = jnp.where(last_hour, jnp.zeros_like(half_energy), half_energy)
    load_total = jnp.sum(load, axis=1)
    gen_now, stor_now = gen_start, stor_start
    gen_old, stor_old = gen_start, stor_start
    price_level, dual_flow, dual_store = lam_start, mu_start, omega_start
    for iteration in range(2):
        if iteration == 0:
            gen_mid, stor_mid = gen_now, stor_now
        else:
            gen_mid = gen_now + THETA * (gen_now - gen_old)
            stor_mid = stor_now + THETA * (stor_now - stor_old)
        bus_price = jnp.dot(dual_flow.astype(jnp.bfloat16), ptdf, preferred_element_type=jnp.float32)
        gen_price = jnp.take(bus_price, gen_index, axis=1)
        stor_price = jnp.take(bus_price, stor_global, axis=1)
        gen_grad = 2.0 * gen_quad * gen_mid + gen_lin + price_level[:, None] + gen_price
        gen_next = jnp.clip(gen_mid - TAU * gen_grad, 0.0, gen_max)
        stor_grad = 2.0 * stor_quad * stor_mid + price_level[:, None] + stor_price + reverse_cum(dual_store, HOURS)
        stor_next = jnp.clip(stor_mid - TAU * stor_grad, -stor_rate, stor_rate)
        gen_bar = 2.0 * gen_next - gen_now
        stor_bar = 2.0 * stor_next - stor_now
        gen_inject = jax.ops.segment_sum(gen_bar.T, gen_index, num_segments=BUSES).T
        stor_inject = jax.ops.segment_sum(stor_bar.T, stor_global, num_segments=BUSES).T
        injection = gen_inject + stor_inject - load
        flow_sum = jnp.dot(injection.astype(jnp.bfloat16), ptdf.T, preferred_element_type=jnp.float32)
        dual_flow = dual_step(dual_flow, flow_sum, SIGMA_FLOW, -limit, limit)
        balance = jnp.sum(gen_bar, axis=1) + jnp.sum(stor_bar, axis=1) - load_total
        price_level = price_level + (KAPPA / (GENS + STOR)) * balance
        dual_store = dual_step(dual_store, forward_cum(stor_bar, HOURS), SIGMA_STORE, low_bound, high_bound)
        gen_old, stor_old = gen_now, stor_now
        gen_now, stor_now = gen_next, stor_next
    return gen_now, stor_now, price_level, dual_flow, dual_store
```

```python
import functools
import jax
import jax.numpy as jnp
from jax import lax
from jax.experimental import pallas as pl
from jax.experimental.pallas import tpu as pltpu
from jax.sharding import PartitionSpec as P

HOURS = 24
TAU = 0.25
SIGMA_FLOW = 4.0
SIGMA_STORE = 0.25
KAPPA = 1.0
THETA = 0.5

F32 = jnp.float32
BF16 = jnp.bfloat16
MESH = pl.DeviceIdType.MESH
DRAIN = 12
POOL = 40
ORDER = (
    "f0 p0 l0 g0",
    "m0 f1 p1 f2",
    "p2 u0 m1 a0",
    "m2 u1 a1 d0",
    "u2 a2 d1 f0",
    "p0 d2 m0 f1",
    "p1 u0 f2 a0",
    "p2 m1 m2 u1",
    "a1 d0 u2 a2",
    "r0 d1 r1 r2",
    "s0 s1 d2 s2",
)
HIGHEST = lax.Precision.HIGHEST


def nt(a, b, precision=None):
    return lax.dot_general(
        a, b, (((1,), (1,)), ((), ())), preferred_element_type=F32, precision=precision
    )


def nn(a, b, precision=None):
    return lax.dot_general(
        a, b, (((1,), (0,)), ((), ())), preferred_element_type=F32, precision=precision
    )


def iota(shape, dim):
    return lax.broadcasted_iota(jnp.int32, shape, dim)


def eye(n):
    return iota((n, n), 0) == iota((n, n), 1)


def summed(x, mask):
    high = x.astype(BF16)
    rest = x - high.astype(F32)
    mid = rest.astype(BF16)
    low = (rest - mid.astype(F32)).astype(BF16)
    return nn(high, mask) + (nn(mid, mask) + nn(low, mask))


def masked_sum(mask, x):
    high = x.astype(BF16)
    rest = x - high.astype(F32)
    mid = rest.astype(BF16)
    low = (rest - mid.astype(F32)).astype(BF16)
    mask = mask.astype(BF16)
    return nn(mask, high) + (nn(mask, mid) + nn(mask, low))


def flipped(x):
    if x.shape[0] % 128 == 0 and x.shape[1] % 128 == 0:
        return x.T
    return nt(eye(x.shape[1]).astype(F32), x, HIGHEST)


def to_column(row):
    n = row.shape[1]
    return jnp.sum(jnp.where(eye(n), row, 0.0), axis=1, keepdims=True)


def to_row(column):
    n = column.shape[0]
    return jnp.sum(jnp.where(eye(n), column, 0.0), axis=0, keepdims=True)


def remote_copy(src, dst, send_sem, recv_sem, target):
    return pltpu.make_async_remote_copy(
        src_ref=src,
        dst_ref=dst,
        send_sem=send_sem,
        recv_sem=recv_sem,
        device_id=target,
        device_id_type=MESH,
    )


class Sent:
    def __init__(self, copy, slot):
        self.copy = copy
        self.slot = slot

    def start(self):
        self.copy.start()

    def wait_send(self):
        self.copy.wait_send()

    def wait_recv(self):
        self.copy.wait_recv()


class Guarded:
    def __init__(self, copy, sends, receives):
        self.copy = copy
        self.slot = copy.slot
        self.sends = sends
        self.receives = receives

    def start(self):
        pl.when(self.sends)(lambda: self.copy.start())

    def wait_send(self):
        pl.when(self.sends)(lambda: self.copy.wait_send())

    def wait_recv(self):
        pl.when(self.receives)(lambda: self.copy.wait_recv())


def flip_bits(value, mask):
    bit = 1
    while bit <= mask:
        if mask // bit % 2:
            value = value + (1 - 2 * ((value // bit) % 2)) * bit
        bit *= 2
    return value


def kernel(
    lines_n,
    buses_n,
    slots,
    gen_bus,
    mu_in_hbm,
    ratings_hbm,
    line_index,
    gen_quad,
    gen_lin,
    gen_max,
    gen_start_hbm,
    stor_bus,
    stor_quad,
    stor_rate,
    stor_energy,
    stor_start_hbm,
    lam_in,
    omega_in_hbm,
    ptdf_hbm,
    load_hbm,
    gen_out,
    stor_out,
    lam_out,
    mu_out,
    omega_out,
    ptdf,
    load,
    load_low,
    load_flow,
    hits,
    par_send,
    par_all,
    par_turned,
    state_send,
    state_recv,
    a_t,
    a_n,
    dual_all,
    price_half,
    price_send,
    price_recv,
    gen_keep,
    stor_keep,
    bar_keep,
    gen_last,
    ret_all,
    flow_part,
    pair_recv,
    line_part,
    line_recv,
    bal_send,
    bal_recv,
    gen_start,
    stor_start,
    omega_in,
    mu_in,
    ratings,
    in_sem,
    send_sem,
    par_sem,
    state_sem,
    share_sem,
    ag_sem,
    fwd_sem,
    pr_sem,
    pair_sem,
    line_sem,
    bal_sem,
    ret_sem,
    rag_sem,
    back_place,
    gen_part,
    stor_part,
    lam_part,
    mu_part,
    omega_part,
):
    rows = load.shape[0]
    line_count, bus_count = ptdf.shape
    gens = gen_bus.shape[1]
    stors = stor_bus.shape[1]
    share = mu_in.shape[1]
    chips = buses_n // 2
    width = buses_n * slots
    units = width + stors
    half = line_count // 2
    blocks = buses_n // lines_n
    turns = price_send.shape[2]
    total_units = (gens + stors) * buses_n
    i = lax.axis_index("lines")
    j = lax.axis_index("buses")
    z = j // 2
    c = j % 2
    partner = (i, z * 2 + (1 - c))
    masks = list(range(1, chips))
    mine_now = j % lines_n == i
    chunk = dual_all.shape[-1]
    chunks = rows // chunk

    def cut(n):
        return slice(n * chunk, (n + 1) * chunk)

    load_copy = pltpu.make_async_copy(load_hbm, load, in_sem.at[0])
    ptdf_copy = pltpu.make_async_copy(ptdf_hbm, ptdf, in_sem.at[1])
    small_copies = [
        pltpu.make_async_copy(source, into, in_sem.at[2 + n])
        for n, (source, into) in enumerate(
            (
                (mu_in_hbm, mu_in),
                (gen_start_hbm, gen_start),
                (ratings_hbm, ratings),
                (stor_start_hbm, stor_start),
                (omega_in_hbm, omega_in),
            )
        )
    ]
    for copy in small_copies:
        copy.start()
    ptdf_copy.start()
    load_copy.start()

    barrier = pltpu.get_barrier_semaphore()
    for off in range(1, buses_n):
        pl.semaphore_signal(
            barrier, inc=1, device_id=(i, lax.rem(j + off, buses_n)), device_id_type=MESH
        )
    for off in range(1, lines_n):
        pl.semaphore_signal(
            barrier, inc=1, device_id=(lax.rem(i + off, lines_n), j), device_id_type=MESH
        )

    bus = gen_bus[...]
    target = bus // bus_count
    target_hit = iota((buses_n, gens), 0) == target
    upto = (iota((gens, gens), 0) <= iota((gens, gens), 1)).astype(BF16)
    count = nn(target_hit.astype(BF16), upto)
    rank = jnp.sum(jnp.where(target_hit, count, 0.0), axis=0, keepdims=True).astype(jnp.int32) - 1
    place = (iota((width, gens), 0) == target * slots + rank).astype(BF16)
    params = jnp.concatenate(
        [(bus - target * bus_count + 1).astype(F32), gen_quad[...], gen_lin[...], gen_max[...]], axis=0
    )
    high = params.astype(BF16)
    rest = params - high.astype(F32)
    mid = rest.astype(BF16)
    low = (rest - mid.astype(F32)).astype(BF16)
    par_send[...] = nt(high, place) + (nt(mid, place) + nt(low, place))
    par_all[j] = par_send[...]

    small_copies[0].wait()
    mu = flipped(mu_in[...])
    for n in range(chunks):
        dual_all[0, n, c, z] = mu[:, cut(n)].astype(BF16)
    small_copies[1].wait()
    state = nt(place, gen_start[...].astype(BF16)).astype(BF16)
    state_send[...] = state.reshape(buses_n, slots, rows)

    @pl.when(mine_now)
    def _():
        state_recv[i, j // lines_n] = state_send[j]

    pl.semaphore_wait(barrier, buses_n + lines_n - 2)

    started = []
    stage_count = [0]

    holders = {}

    def remote(source, into, arrived, target):
        slot = min(range(POOL), key=lambda s: holders[s][0] if s in holders else -1)
        if slot in holders and holders[slot][1] in started:
            started.remove(holders[slot][1])
            holders[slot][1][1].wait_send()
        holders[slot] = (len(holders) and max(h[0] for h in holders.values()) + 1, None)
        return Sent(remote_copy(source, into, send_sem.at[slot], arrived, target), slot)

    def go(copy):
        copy.start()
        entry = (stage_count[0], copy)
        started.append(entry)
        holders[copy.slot] = (holders[copy.slot][0], entry)
        return copy

    def drain(age):
        stage_count[0] += 1
        while started and started[0][0] + age <= stage_count[0]:
            started.pop(0)[1].wait_send()

    par_copies = []
    for off in range(1, buses_n):
        to = (i, lax.rem(j + off, buses_n))
        par_copies.append(
            go(remote(par_send, par_all.at[j], par_sem.at[off - 1], to))
        )

    def gather_start(k, n):
        mine = dual_all.at[k, n, c, z]
        copies = []
        for off in masks:
            copies.append(
                go(
                    remote(
                        mine,
                        mine,
                        ag_sem.at[n, off],
                        (i, flip_bits(z, off) * 2 + c),
                    )
                )
            )
        copies.append(go(remote(mine, mine, ag_sem.at[n, 0], partner)))
        return copies

    gather = [gather_start(0, 0)]

    stor_column = to_column(stor_bus[...].astype(F32)).astype(jnp.int32)
    hits[width:, :] = (iota((stors, bus_count), 1) == stor_column).astype(BF16)
    for copy in small_copies[2:]:
        copy.wait()
    load_copy.wait()
    load_value = load[...]
    load_total = jnp.sum(load_value, axis=1, keepdims=True)
    load_total = [to_row(load_total[cut(n), :]) for n in range(chunks)]
    load_low[...] = load_value.astype(BF16)
    ptdf_copy.wait()
    wide = max(512, 2 * share) if line_count % 512 == 0 else max(256, 2 * share)
    group = wide // (2 * share)
    step = wide // 2

    def lines_of(t, w):
        block = ptdf[pl.ds(pl.multiple_of(t * wide, wide), wide), :]
        return block.reshape(group, 2, share, bus_count)[:, w].reshape(step, bus_count)

    def load_step(t, carry):
        at = pl.multiple_of(t * step, step)
        for w in range(2):
            load_flow[w, pl.ds(at, step), :] = nt(lines_of(t, w), load_low[...])
        return carry

    lax.fori_loop(0, line_count // wide, load_step, 0)
    for n in range(1, min(2, chunks)):
        gather.append(gather_start(0, n))
    state_copies = []
    for off in range(1, buses_n):
        to = lax.rem(j + off, buses_n)
        source = lax.rem(j - off + buses_n, buses_n)
        state_copies.append(
            go(
                Guarded(
                    remote(
                        state_send.at[to],
                        state_recv.at[i, j // lines_n],
                        state_sem.at[off - 1],
                        (i, to),
                    ),
                    mine_now,
                    source % lines_n == i,
                )
            )
        )

    hold = {"mu": [mu[:, cut(n)] for n in range(chunks)]}
    wanted = jnp.sum(
        jnp.where(iota((buses_n, share), 0) == j, line_index[...].astype(F32), 0.0),
        axis=0,
        keepdims=True,
    )
    wanted = to_column(wanted).astype(jnp.int32)
    lanes = ratings.shape[1]
    high_hit = (iota((share, ratings.shape[0]), 1) == wanted // lanes).astype(F32)
    rated = masked_sum(high_hit, ratings[...])
    hold["limit"] = jnp.sum(
        jnp.where(iota((share, lanes), 1) == wanted % lanes, rated, 0.0), axis=1, keepdims=True
    )
    hold["omega"] = flipped(omega_in[...])
    row_id, col_id = (iota((rows, rows), 0), iota((rows, rows), 1))
    same = row_id // HOURS == col_id // HOURS
    hold["later"] = jnp.where(same & (row_id >= col_id), 1.0, 0.0).astype(BF16)
    hold["earlier"] = jnp.where(same & (row_id <= col_id), 1.0, 0.0).astype(BF16)
    hold["back"] = summed(hold["omega"], hold["later"])
    hold["stor"] = flipped(stor_start[...])
    lam_row = lam_in[...].reshape(1, rows)
    hold["lam"] = [lam_row[:, cut(n)] for n in range(chunks)]
    hold["quad"] = to_column(stor_quad[...])
    hold["rate"] = to_column(stor_rate[...])
    hour = iota((1, rows), 1) % HOURS
    hold["high"] = jnp.where(hour == HOURS - 1, 0.0, to_column(0.5 * stor_energy[...]))

    for copy in par_copies:
        copy.wait_recv()
    every = jnp.concatenate([par_all[a] for a in range(buses_n)], axis=0)
    par_turned[...] = every.T
    mine = par_turned[pl.ds(pl.multiple_of(j * slots, slots), slots), :]

    owners = [q * lines_n + g for g in range(lines_n) for q in range(blocks)]

    def slot_column(p):
        return jnp.concatenate([mine[:, a * 4 + p : a * 4 + p + 1] for a in owners], axis=0)

    slot_bus = slot_column(0).astype(jnp.int32) - 1
    slot_quad, slot_lin, slot_max = (slot_column(1), slot_column(2), slot_column(3))
    hits[:width, :] = (iota((width, bus_count), 1) == slot_bus).astype(BF16)

    def turn_step(t, carry):
        at = pl.multiple_of(t * step, step)
        for w in range(2):
            a_t[w, :, pl.ds(at, step)] = nt(hits[...], lines_of(t, w)).astype(BF16)
        return carry

    for n in range(2, chunks):
        gather.append(gather_start(0, n))
    lax.fori_loop(0, line_count // wide, turn_step, 0)

    def late_setup():
        def flow_step(t, carry):
            at = pl.multiple_of(t * step, step)
            for w in range(2):
                a_n[w, pl.ds(at, step), :] = nt(lines_of(t, w), hits[...]).astype(BF16)
            return carry

        lax.fori_loop(0, line_count // wide, flow_step, 0)
        spot = ((target % lines_n) * blocks + target // lines_n) * slots + rank
        back_place[...] = (iota((width, gens), 0) == spot).astype(BF16)

    pending = {}

    state_shared = []

    def share_state():
        for copy in state_copies:
            copy.wait_recv()
        for off in range(1, lines_n):
            state_shared.append(
                go(
                    remote(
                        state_recv.at[i],
                        state_recv.at[i],
                        share_sem.at[off - 1],
                        (lax.rem(i + off, lines_n), j),
                    )
                )
            )

    def forward_stage(k, n):
        copies = gather[n]
        forwards = [copies[-1]]
        for off, copy in zip(masks, copies):
            copy.wait_recv()
            slot = dual_all.at[k, n, c, flip_bits(z, off)]
            forwards.append(
                go(remote(slot, slot, fwd_sem.at[n, off - 1], partner))
            )
        gather[n] = forwards
        price_half[n] = nn(a_t[c], dual_all[k, n, c].reshape(half, chunk))

    def price_stage(k, n):
        for copy in gather[n]:
            copy.wait_recv()
        value = price_half[n] + nn(a_t[1 - c], dual_all[k, n, 1 - c].reshape(half, chunk))
        price_send[k, n, 0] = value.astype(BF16)
        price_go(k, n, 0)

    def price_go(k, n, turn):
        copies = []
        for h in range(2):
            bit = turn if h == 0 else turns - 1 - turn
            to = i + (1 - 2 * ((i // 2**bit) % 2)) * 2**bit
            at = slice(h * (units // 2), (h + 1) * (units // 2))
            copies.append(
                go(
                    remote(
                        price_send.at[k, n, turn, at],
                        price_recv.at[k, n, turn, at],
                        pr_sem.at[n, turn, h],
                        (to, j),
                    )
                )
            )
        pending[n] = copies

    def mix_stage(turn, k, n):
        for h in range(2):
            pending[n][h].wait_recv()
        value = price_send[k, n, turn - 1].astype(F32) + price_recv[k, n, turn - 1].astype(F32)
        price_send[k, n, turn] = value.astype(BF16)
        price_go(k, n, turn)

    bal_copies = []
    returns = {}
    writes = []

    def write(source, into, which, n):
        copy = pltpu.make_async_copy(source, into, in_sem.at[len(writes)])
        copy.start()
        writes.append(copy)

    def take_balance(k):
        for copy in bal_copies:
            copy.wait_recv()
        bal_copies.clear()
        balance = bal_recv[k, 0]
        for a in range(1, buses_n):
            balance = balance + bal_recv[k, a]
        for n in range(chunks):
            hold["lam"][n] = hold["lam"][n] + (KAPPA / total_units) * balance[:, cut(n)]

    def update_stage(k, n):
        if k == 0 and n == 0:
            for copy in state_shared:
                copy.wait_recv()
        gen_0 = state_recv[:, :, :, cut(n)].reshape(width, chunk).astype(F32)
        stor_0 = hold["stor"][:, cut(n)]
        if k == 0:
            gen_now, stor_now = (gen_0, stor_0)
            gen_mid, stor_mid = (gen_0, stor_0)
        else:
            if n == 0:
                take_balance(0)
            gen_now, stor_now = (gen_keep[:, cut(n)], stor_keep[:, cut(n)])
            gen_mid = gen_now + THETA * (gen_now - gen_0)
            stor_mid = stor_now + THETA * (stor_now - stor_0)
        for copy in pending[n]:
            copy.wait_recv()
        price = price_send[k, n, turns - 1].astype(F32) + price_recv[k, n, turns - 1].astype(F32)
        lam = hold["lam"][n]
        gen_grad = 2.0 * slot_quad * gen_mid + slot_lin + lam + price[:width]
        gen_next = jnp.clip(gen_mid - TAU * gen_grad, 0.0, slot_max)
        stor_grad = 2.0 * hold["quad"] * stor_mid + lam + price[width:] + hold["back"][:, cut(n)]
        stor_next = jnp.clip(stor_mid - TAU * stor_grad, -hold["rate"], hold["rate"])
        gen_bar = 2.0 * gen_next - gen_now
        stor_bar = 2.0 * stor_next - stor_now
        bar_low = jnp.concatenate([gen_bar.astype(BF16), stor_bar.astype(BF16)], axis=0)

        def flow_half(w):
            value = nn(a_n[w], bar_low) - load_flow[w, :, cut(n)]
            flow_part[k, n, w] = value.astype(BF16).reshape(chips, share, chunk)

        flow_half(1 - c)
        pending[n] = go(
            remote(
                flow_part.at[k, n, 1 - c],
                pair_recv.at[k, n],
                pair_sem.at[n],
                partner,
            )
        )
        flow_half(c)
        bal_send[k, :, cut(n)] = (
            jnp.sum(gen_bar, axis=0, keepdims=True)
            + jnp.sum(stor_bar, axis=0, keepdims=True)
            - load_total[n]
        )
        bar_keep[:, cut(n)] = stor_bar
        if k == 0:
            gen_keep[:, cut(n)] = gen_next
            stor_keep[:, cut(n)] = stor_next
        else:
            gen_last[:, :, :, cut(n)] = gen_next.astype(BF16).reshape(lines_n, blocks, slots, chunk)
            returns[n] = []
            for off in range(1, buses_n):
                to = lax.rem(j + off, buses_n)
                source = lax.rem(j - off + buses_n, buses_n)
                returns[n].append(
                    go(
                        Guarded(
                            remote(
                                gen_last.at[to % lines_n, to // lines_n, :, cut(n)],
                                ret_all.at[n, i, j // lines_n],
                                ret_sem.at[n, off - 1],
                                (i, to),
                            ),
                            mine_now,
                            source % lines_n == i,
                        )
                    )
                )

            @pl.when(mine_now)
            def _():
                ret_all[n, i, j // lines_n] = gen_last[i, j // lines_n, :, cut(n)]

            stor_part[cut(n), :] = flipped(stor_next)
            write(stor_part.at[cut(n)], stor_out.at[cut(n)], 1, n)
        if n < chunks - 1:
            return
        bal_recv[k, j] = bal_send[k]
        for off in range(1, buses_n):
            bal_copies.append(
                go(
                    remote(
                        bal_send.at[k],
                        bal_recv.at[k, j],
                        bal_sem.at[k, off - 1],
                        (i, lax.rem(j + off, buses_n)),
                    )
                )
            )

    def pair_stage(k, n):
        pending[n].wait_recv()
        copies = []
        for off in masks:
            to = flip_bits(z, off)
            value = flow_part[k, n, c, to].astype(F32) + pair_recv[k, n, to].astype(F32)
            line_part[k, n, off] = value.astype(BF16)
            copies.append(
                go(
                    remote(
                        line_part.at[k, n, off],
                        line_recv.at[k, n, off],
                        line_sem.at[n, off - 1],
                        (i, to * 2 + c),
                    )
                )
            )
        pending[n] = copies
        if n == chunks - 1:
            charge = summed(bar_keep[...], hold["earlier"])
            shifted = hold["omega"] + SIGMA_STORE * charge
            high = hold["high"]
            omega = shifted - SIGMA_STORE * jnp.clip(shifted / SIGMA_STORE, -high, high)
            if k == 0:
                hold["omega"] = omega
                hold["back"] = summed(omega, hold["later"])
            else:
                omega_part[...] = flipped(omega)
                write(omega_part, omega_out, 3, 0)

    def dual_stage(k, n):
        flow = flow_part[k, n, c, z].astype(F32) + pair_recv[k, n, z].astype(F32)
        for off, copy in zip(masks, pending[n]):
            copy.wait_recv()
            flow = flow + line_recv[k, n, off].astype(F32)
        shifted = hold["mu"][n] + SIGMA_FLOW * flow
        limit = hold["limit"]
        mu = shifted - SIGMA_FLOW * jnp.clip(shifted / SIGMA_FLOW, -limit, limit)
        if k == 0:
            hold["mu"][n] = mu
            dual_all[1, n, c, z] = mu.astype(BF16)
            gather[n] = gather_start(1, n)
        else:
            mu_part[cut(n), :] = flipped(mu)
            write(mu_part.at[cut(n)], mu_out.at[cut(n)], 2, n)

    def return_stage(n):
        for copy in returns[n]:
            copy.wait_recv()
        returns[n] = []
        for off in range(1, lines_n):
            returns[n].append(
                go(
                    remote(
                        ret_all.at[n, i],
                        ret_all.at[n, i],
                        rag_sem.at[n, off - 1],
                        (lax.rem(i + off, lines_n), j),
                    )
                )
            )

    def result_stage(n):
        for copy in returns[n]:
            copy.wait_recv()
        gen_part[cut(n), :] = lax.dot_general(
            ret_all[n].reshape(width, chunk),
            back_place[...],
            (((0,), (0,)), ((), ())),
            preferred_element_type=F32,
        )
        write(gen_part.at[cut(n)], gen_out.at[cut(n)], 0, n)

    kinds = [("f", forward_stage), ("p", price_stage)]
    for turn in range(1, turns):
        kinds.append(("m", functools.partial(mix_stage, turn)))
    kinds += [("u", update_stage), ("a", pair_stage), ("d", dual_stage)]
    stages = [(kind, functools.partial(stage, k)) for k in range(2) for kind, stage in kinds]
    tail = [("r", return_stage), ("s", result_stage)]
    queue = [list(stages) for n in range(chunks)]
    ends = [list(tail) for n in range(chunks)]
    if chunks == 3 and turns == 2:
        order = " ".join(ORDER).split()
    else:
        order = ["l0", "g0"] + [kind + str(n) for kind, _ in stages + tail for n in range(chunks)]
    for entry in order:
        kind, n = (entry[0], int(entry[1:]))
        if kind == "l":
            stage = lambda n: late_setup()
        elif kind == "g":
            stage = lambda n: share_state()
        else:
            kind, stage = (ends if kind in "rs" else queue)[n].pop(0)
        stage(n)
        drain(DRAIN)
    take_balance(1)
    lam_part[...] = jnp.concatenate(hold["lam"], axis=1)
    write(lam_part, lam_out, 3, 1)
    for copy in writes:
        copy.wait()
    drain(0)


def finish(*refs):
    count = len(refs) // 2
    for source, result in zip(refs[:count], refs[count:]):
        result[...] = source[...].reshape(result.shape)


def shards(
    ptdf,
    load,
    ratings,
    line_index,
    gen_bus,
    gen_quad,
    gen_lin,
    gen_max,
    gen_start,
    stor_bus,
    stor_quad,
    stor_rate,
    stor_energy,
    stor_start,
    lam_start,
    mu_start,
    omega_start,
):
    lines_n = lax.axis_size("lines")
    buses_n = lax.axis_size("buses")
    rows, bus_count = load.shape
    line_count = ptdf.shape[0]
    gens = gen_bus.shape[0]
    stors = stor_bus.shape[0]
    share = line_count // buses_n
    chips = buses_n // 2
    slots = max(8, (gens + buses_n - 1) // buses_n)
    slots = (slots + 15) // 16 * 16
    width = buses_n * slots
    units = width + stors
    blocks = buses_n // lines_n
    turns = lines_n.bit_length() - 1
    half = line_count // 2
    chunk = 128 if rows % 128 == 0 else rows
    chunks = rows // chunk
    vmem = pl.BlockSpec(memory_space=pltpu.VMEM)
    hbm = pl.BlockSpec(memory_space=pl.ANY)
    dma = pltpu.SemaphoreType.DMA
    outs = pl.pallas_call(
        functools.partial(kernel, lines_n, buses_n, slots),
        out_shape=(
            jax.ShapeDtypeStruct((rows, gens), F32),
            jax.ShapeDtypeStruct((rows, stors), F32),
            jax.ShapeDtypeStruct((1, rows), F32),
            jax.ShapeDtypeStruct((rows, share), F32),
            jax.ShapeDtypeStruct((rows, stors), F32),
        ),
        in_specs=[hbm if n in (1, 2, 7, 12, 14, 15, 16) else vmem for n in range(17)],
        out_specs=(hbm,) * 5,
        scratch_shapes=[
            pltpu.VMEM((line_count, bus_count), BF16),
            pltpu.VMEM((rows, bus_count), F32),
            pltpu.VMEM((rows, bus_count), BF16),
            pltpu.VMEM((2, half, rows), F32),
            pltpu.VMEM((units, bus_count), BF16),
            pltpu.VMEM((4, width), F32),
            pltpu.VMEM((buses_n, 4, width), F32),
            pltpu.VMEM((width, buses_n * 4), F32),
            pltpu.VMEM((buses_n, slots, rows), BF16),
            pltpu.VMEM((lines_n, blocks, slots, rows), BF16),
            pltpu.VMEM((2, units, half), BF16),
            pltpu.VMEM((2, half, units), BF16),
            pltpu.VMEM((2, chunks, 2, chips, share, chunk), BF16),
            pltpu.VMEM((chunks, units, chunk), F32),
            pltpu.VMEM((2, chunks, turns, units, chunk), BF16),
            pltpu.VMEM((2, chunks, turns, units, chunk), BF16),
            pltpu.VMEM((width, rows), F32),
            pltpu.VMEM((stors, rows), F32),
            pltpu.VMEM((stors, rows), F32),
            pltpu.VMEM((lines_n, blocks, slots, rows), BF16),
            pltpu.VMEM((chunks, lines_n, blocks, slots, chunk), BF16),
            pltpu.VMEM((2, chunks, 2, chips, share, chunk), BF16),
            pltpu.VMEM((2, chunks, chips, share, chunk), BF16),
            pltpu.VMEM((2, chunks, chips, share, chunk), BF16),
            pltpu.VMEM((2, chunks, chips, share, chunk), BF16),
            pltpu.VMEM((2, 1, rows), F32),
            pltpu.VMEM((2, buses_n, 1, rows), F32),
            pltpu.VMEM((rows, gens), F32),
            pltpu.VMEM((rows, stors), F32),
            pltpu.VMEM((rows, stors), F32),
            pltpu.VMEM((rows, share), F32),
            pltpu.VMEM((ratings.shape[0] // 128, 128), F32),
            dma((max(7, 3 * chunks + 2),)),
            dma((POOL,)),
            dma((buses_n - 1,)),
            dma((buses_n - 1,)),
            dma((lines_n - 1,)),
            dma((chunks, chips)),
            dma((chunks, chips - 1)),
            dma((chunks, turns, 2)),
            dma((chunks,)),
            dma((chunks, chips - 1)),
            dma((2, buses_n - 1)),
            dma((chunks, buses_n - 1)),
            dma((chunks, lines_n - 1)),
            pltpu.VMEM((width, gens), BF16),
            pltpu.VMEM((rows, gens), F32),
            pltpu.VMEM((rows, stors), F32),
            pltpu.VMEM((1, rows), F32),
            pltpu.VMEM((rows, share), F32),
            pltpu.VMEM((rows, stors), F32),
        ],
        compiler_params=pltpu.CompilerParams(
            collective_id=0, has_side_effects=True, vmem_limit_bytes=60 * 1024 * 1024
        ),
    )(
        gen_bus[None, :],
        mu_start,
        ratings.reshape(-1, 128),
        line_index.reshape(buses_n, share),
        gen_quad[None, :],
        gen_lin[None, :],
        gen_max[None, :],
        gen_start,
        stor_bus[None, :],
        stor_quad[None, :],
        stor_rate[None, :],
        stor_energy[None, :],
        stor_start,
        lam_start,
        omega_start,
        ptdf,
        load,
    )
    shapes = [x.shape for x in outs]
    shapes[2] = (rows,)
    return pl.pallas_call(
        finish,
        out_shape=tuple(jax.ShapeDtypeStruct(shape, F32) for shape in shapes),
        in_specs=[vmem] * 5,
        out_specs=(vmem,) * 5,
    )(*outs)


def solution(mesh):
    return jax.shard_map(
        shards,
        mesh=mesh,
        in_specs=(
            P("lines", "buses"),
            P(None, "buses"),
            P(),
            P("lines"),
            P("buses"),
            P("buses"),
            P("buses"),
            P("buses"),
            P(None, "buses"),
            P("buses"),
            P("buses"),
            P("buses"),
            P("buses"),
            P(None, "buses"),
            P(),
            P(None, ("lines", "buses")),
            P(None, "buses"),
        ),
        out_specs=(
            P(None, "buses"),
            P(None, "buses"),
            P(),
            P(None, ("lines", "buses")),
            P(None, "buses"),
        ),
        check_vma=False,
    )
```

```python
import functools
import jax
import jax.numpy as jnp
from jax import lax
from jax.experimental import pallas as pl
from jax.experimental.pallas import tpu as pltpu
from jax.sharding import PartitionSpec as P

HOURS = 24
TAU = 0.25
SIGMA_FLOW = 4.0
SIGMA_STORE = 0.25
KAPPA = 1.0
THETA = 0.5

F32 = jnp.float32
BF16 = jnp.bfloat16
MESH = pl.DeviceIdType.MESH
DRAIN = 12
POOL = 30
ORDER = (
    "f0 p0 l0 m0",
    "f1 p1 f2 p2",
    "u0 m1 m2 a0",
    "u1 a1 d0 u2",
    "a2 d1 f0 p0",
    "d2 f1 m0 p1",
    "f2 u0 p2 a0",
    "m1 m2 u1 a1",
    "d0 u2 a2 r0",
    "r1 d1 r2 s0",
    "s1 d2 s2",
)
HIGHEST = lax.Precision.HIGHEST


def nt(a, b, precision=None):
    return lax.dot_general(
        a, b, (((1,), (1,)), ((), ())), preferred_element_type=F32, precision=precision
    )


def nn(a, b, precision=None):
    return lax.dot_general(
        a, b, (((1,), (0,)), ((), ())), preferred_element_type=F32, precision=precision
    )


def iota(shape, dim):
    return lax.broadcasted_iota(jnp.int32, shape, dim)


def eye(n):
    return iota((n, n), 0) == iota((n, n), 1)


def summed(x, mask):
    high = x.astype(BF16)
    rest = x - high.astype(F32)
    mid = rest.astype(BF16)
    low = (rest - mid.astype(F32)).astype(BF16)
    return nn(high, mask) + (nn(mid, mask) + nn(low, mask))


def masked_sum(mask, x):
    high = x.astype(BF16)
    rest = x - high.astype(F32)
    mid = rest.astype(BF16)
    low = (rest - mid.astype(F32)).astype(BF16)
    mask = mask.astype(BF16)
    return nn(mask, high) + (nn(mask, mid) + nn(mask, low))


def flipped(x):
    if x.shape[0] % 128 == 0 and x.shape[1] % 128 == 0:
        return x.T
    return nt(eye(x.shape[1]).astype(F32), x, HIGHEST)


def to_column(row):
    n = row.shape[1]
    return jnp.sum(jnp.where(eye(n), row, 0.0), axis=1, keepdims=True)


def to_row(column):
    n = column.shape[0]
    return jnp.sum(jnp.where(eye(n), column, 0.0), axis=0, keepdims=True)


def remote_copy(src, dst, send_sem, recv_sem, target):
    return pltpu.make_async_remote_copy(
        src_ref=src,
        dst_ref=dst,
        send_sem=send_sem,
        recv_sem=recv_sem,
        device_id=target,
        device_id_type=MESH,
    )


class Sent:
    def __init__(self, copy, slot):
        self.copy = copy
        self.slot = slot

    def start(self):
        self.copy.start()

    def wait_send(self):
        self.copy.wait_send()

    def wait_recv(self):
        self.copy.wait_recv()


class Guarded:
    def __init__(self, copy, sends, receives):
        self.copy = copy
        self.slot = copy.slot
        self.sends = sends
        self.receives = receives

    def start(self):
        pl.when(self.sends)(lambda: self.copy.start())

    def wait_send(self):
        pl.when(self.sends)(lambda: self.copy.wait_send())

    def wait_recv(self):
        pl.when(self.receives)(lambda: self.copy.wait_recv())


def flip_bits(value, mask):
    bit = 1
    while bit <= mask:
        if mask // bit % 2:
            value = value + (1 - 2 * ((value // bit) % 2)) * bit
        bit *= 2
    return value


def kernel(
    lines_n,
    buses_n,
    slots,
    gen_bus,
    mu_in_hbm,
    ratings_hbm,
    line_index,
    gen_quad,
    gen_lin,
    gen_max,
    gen_start_hbm,
    stor_bus,
    stor_quad,
    stor_rate,
    stor_energy,
    stor_start_hbm,
    lam_in,
    omega_in_hbm,
    ptdf_hbm,
    load_hbm,
    gen_out,
    stor_out,
    lam_out,
    mu_out,
    omega_out,
    ptdf,
    load,
    load_low,
    load_flow,
    hits,
    par_send,
    par_all,
    par_turned,
    state_send,
    state_recv,
    a_t,
    a_n,
    dual_all,
    price_half,
    price_send,
    price_recv,
    gen_keep,
    stor_keep,
    bar_keep,
    gen_last,
    ret_all,
    flow_part,
    pair_recv,
    line_part,
    line_recv,
    bal_send,
    bal_recv,
    gen_start,
    stor_start,
    omega_in,
    mu_in,
    ratings,
    in_sem,
    send_sem,
    par_sem,
    state_sem,
    share_sem,
    ag_sem,
    fwd_sem,
    pr_sem,
    pair_sem,
    line_sem,
    ret_sem,
    rag_sem,
    back_place,
    gen_part,
    stor_part,
    lam_part,
    mu_part,
    omega_part,
):
    rows = load.shape[0]
    line_count, bus_count = ptdf.shape
    gens = gen_bus.shape[1]
    stors = stor_bus.shape[1]
    share = mu_in.shape[1]
    chips = buses_n // 2
    width = buses_n * slots
    units = width + stors
    half = line_count // 2
    blocks = buses_n // lines_n
    turns = price_send.shape[2]
    total_units = (gens + stors) * buses_n
    i = lax.axis_index("lines")
    j = lax.axis_index("buses")
    z = j // 2
    c = j % 2
    partner = (i, z * 2 + (1 - c))
    masks = list(range(1, chips))
    mine_now = j % lines_n == i
    chunk = dual_all.shape[-1]
    chunks = rows // chunk

    def cut(n):
        return slice(n * chunk, (n + 1) * chunk)

    load_copy = pltpu.make_async_copy(load_hbm, load, in_sem.at[0])
    ptdf_copy = pltpu.make_async_copy(ptdf_hbm, ptdf, in_sem.at[1])
    small_copies = [
        pltpu.make_async_copy(source, into, in_sem.at[2 + n])
        for n, (source, into) in enumerate(
            (
                (mu_in_hbm, mu_in),
                (gen_start_hbm, gen_start),
                (ratings_hbm, ratings),
                (stor_start_hbm, stor_start),
                (omega_in_hbm, omega_in),
            )
        )
    ]
    for copy in small_copies:
        copy.start()
    ptdf_copy.start()
    load_copy.start()

    barrier = pltpu.get_barrier_semaphore()
    for off in range(1, buses_n):
        pl.semaphore_signal(
            barrier, inc=1, device_id=(i, lax.rem(j + off, buses_n)), device_id_type=MESH
        )
    for off in range(1, lines_n):
        pl.semaphore_signal(
            barrier, inc=1, device_id=(lax.rem(i + off, lines_n), j), device_id_type=MESH
        )

    bus = gen_bus[...]
    target = bus // bus_count
    target_hit = iota((buses_n, gens), 0) == target
    upto = (iota((gens, gens), 0) <= iota((gens, gens), 1)).astype(BF16)
    count = nn(target_hit.astype(BF16), upto)
    rank = jnp.sum(jnp.where(target_hit, count, 0.0), axis=0, keepdims=True).astype(jnp.int32) - 1
    place = (iota((width, gens), 0) == target * slots + rank).astype(BF16)
    params = jnp.concatenate(
        [(bus - target * bus_count + 1).astype(F32), gen_quad[...], gen_lin[...], gen_max[...]], axis=0
    )
    high = params.astype(BF16)
    rest = params - high.astype(F32)
    mid = rest.astype(BF16)
    low = (rest - mid.astype(F32)).astype(BF16)
    par_send[...] = nt(high, place) + (nt(mid, place) + nt(low, place))
    par_all[j] = par_send[...]

    small_copies[0].wait()
    mu = flipped(mu_in[...])
    for n in range(chunks):
        dual_all[0, n, c, z] = mu[:, cut(n)].astype(BF16)
    small_copies[1].wait()
    state = nt(place, gen_start[...].astype(BF16)).astype(BF16)
    for n in range(chunks):
        state_send[n] = state[:, cut(n)].reshape(buses_n, slots, chunk)
    for n in range(chunks):

        @pl.when((j + n) % lines_n == i)
        def _(n=n):
            state_recv[n, j % lines_n, j // lines_n] = state_send[n, j]

    pl.semaphore_wait(barrier, buses_n + lines_n - 2)

    started = []
    stage_count = [0]

    holders = {}

    def remote(source, into, arrived, target):
        slot = min(range(POOL), key=lambda s: holders[s][0] if s in holders else -1)
        if slot in holders and holders[slot][1] in started:
            started.remove(holders[slot][1])
            holders[slot][1][1].wait_send()
        holders[slot] = (len(holders) and max(h[0] for h in holders.values()) + 1, None)
        return Sent(remote_copy(source, into, send_sem.at[slot], arrived, target), slot)

    def go(copy):
        copy.start()
        entry = (stage_count[0], copy)
        started.append(entry)
        holders[copy.slot] = (holders[copy.slot][0], entry)
        return copy

    def drain(age):
        stage_count[0] += 1
        while started and started[0][0] + age <= stage_count[0]:
            started.pop(0)[1].wait_send()

    par_copies = []
    for off in range(1, buses_n):
        to = (i, lax.rem(j + off, buses_n))
        par_copies.append(
            go(remote(par_send, par_all.at[j], par_sem.at[off - 1], to))
        )

    def gather_start(k, n):
        mine = dual_all.at[k, n, c, z]
        copies = []
        for off in masks:
            copies.append(
                go(
                    remote(
                        mine,
                        mine,
                        ag_sem.at[n, off],
                        (i, flip_bits(z, off) * 2 + c),
                    )
                )
            )
        copies.append(go(remote(mine, mine, ag_sem.at[n, 0], partner)))
        return copies

    state_copies = []
    for base in range(0, chunks, lines_n):
        for off in range(1, buses_n):
            to = lax.rem(j + off, buses_n)
            source = lax.rem(j - off + buses_n, buses_n)
            at = base + (i - j + buses_n) % lines_n
            held = jnp.minimum(at, chunks - 1)
            state_copies.append(
                go(
                    Guarded(
                        remote(
                            state_send.at[held, to],
                            state_recv.at[held, j % lines_n, j // lines_n],
                            state_sem.at[base // lines_n, off - 1],
                            (i, to),
                        ),
                        at < chunks,
                        base + (i - source + buses_n) % lines_n < chunks,
                    )
                )
            )
    gather = [gather_start(0, 0)]

    stor_column = to_column(stor_bus[...].astype(F32)).astype(jnp.int32)
    hits[width:, :] = (iota((stors, bus_count), 1) == stor_column).astype(BF16)
    for copy in small_copies[2:]:
        copy.wait()
    load_copy.wait()
    load_value = load[...]
    load_total = jnp.sum(load_value, axis=1, keepdims=True)
    load_total = [to_row(load_total[cut(n), :]) for n in range(chunks)]
    load_low[...] = load_value.astype(BF16)
    ptdf_copy.wait()
    wide = max(512, 2 * share) if line_count % 512 == 0 else max(256, 2 * share)
    group = wide // (2 * share)
    step = wide // 2

    def lines_of(t, w):
        block = ptdf[pl.ds(pl.multiple_of(t * wide, wide), wide), :]
        return block.reshape(group, 2, share, bus_count)[:, w].reshape(step, bus_count)

    def load_step(t, carry):
        at = pl.multiple_of(t * step, step)
        for w in range(2):
            load_flow[w, pl.ds(at, step), :] = nt(lines_of(t, w), load_low[...])
        return carry

    lax.fori_loop(0, line_count // wide, load_step, 0)
    for n in range(1, min(2, chunks)):
        gather.append(gather_start(0, n))
    hold = {"mu": [mu[:, cut(n)] for n in range(chunks)]}
    wanted = jnp.sum(
        jnp.where(iota((buses_n, share), 0) == j, line_index[...].astype(F32), 0.0),
        axis=0,
        keepdims=True,
    )
    wanted = to_column(wanted).astype(jnp.int32)
    lanes = ratings.shape[1]
    high_hit = (iota((share, ratings.shape[0]), 1) == wanted // lanes).astype(F32)
    rated = masked_sum(high_hit, ratings[...])
    hold["limit"] = jnp.sum(
        jnp.where(iota((share, lanes), 1) == wanted % lanes, rated, 0.0), axis=1, keepdims=True
    )
    hold["omega"] = flipped(omega_in[...])
    row_id, col_id = (iota((rows, rows), 0), iota((rows, rows), 1))
    same = row_id // HOURS == col_id // HOURS
    hold["later"] = jnp.where(same & (row_id >= col_id), 1.0, 0.0).astype(BF16)
    hold["earlier"] = jnp.where(same & (row_id <= col_id), 1.0, 0.0).astype(BF16)
    hold["back"] = summed(hold["omega"], hold["later"])
    hold["stor"] = flipped(stor_start[...])
    lam_row = lam_in[...].reshape(1, rows)
    hold["lam"] = [lam_row[:, cut(n)] for n in range(chunks)]
    hold["quad"] = to_column(stor_quad[...])
    hold["rate"] = to_column(stor_rate[...])
    hour = iota((1, rows), 1) % HOURS
    hold["high"] = jnp.where(hour == HOURS - 1, 0.0, to_column(0.5 * stor_energy[...]))

    for copy in par_copies:
        copy.wait_recv()
    every = jnp.concatenate([par_all[a] for a in range(buses_n)], axis=0)
    par_turned[...] = every.T
    mine = par_turned[pl.ds(pl.multiple_of(j * slots, slots), slots), :]

    owners = [q * lines_n + g for g in range(lines_n) for q in range(blocks)]

    def slot_column(p):
        return jnp.concatenate([mine[:, a * 4 + p : a * 4 + p + 1] for a in owners], axis=0)

    slot_bus = slot_column(0).astype(jnp.int32) - 1
    slot_quad, slot_lin, slot_max = (slot_column(1), slot_column(2), slot_column(3))
    hits[:width, :] = (iota((width, bus_count), 1) == slot_bus).astype(BF16)

    def turn_step(t, carry):
        at = pl.multiple_of(t * step, step)
        for w in range(2):
            a_t[w, :, pl.ds(at, step)] = nt(hits[...], lines_of(t, w)).astype(BF16)
        return carry

    state_shared = []

    def share_state():
        for copy in state_copies:
            copy.wait_recv()
        for n in range(chunks):
            state_shared.append([])
            held = state_recv.at[n, (i - n + chunks * lines_n) % lines_n]
            for off in range(1, lines_n):
                to = (lax.rem(i + off, lines_n), j)
                state_shared[n].append(go(remote(held, held, share_sem.at[n, off - 1], to)))

    share_state()
    for n in range(2, chunks):
        gather.append(gather_start(0, n))
    lax.fori_loop(0, line_count // wide, turn_step, 0)

    def late_setup():
        def flow_step(t, carry):
            at = pl.multiple_of(t * step, step)
            for w in range(2):
                a_n[w, pl.ds(at, step), :] = nt(lines_of(t, w), hits[...]).astype(BF16)
            return carry

        lax.fori_loop(0, line_count // wide, flow_step, 0)
        spot = ((target % lines_n) * blocks + target // lines_n) * slots + rank
        back_place[...] = (iota((width, gens), 0) == spot).astype(BF16)

    pending = {}

    def forward_stage(k, n):
        copies = gather[n]
        forwards = [copies[-1]]
        for off, copy in zip(masks, copies):
            copy.wait_recv()
            slot = dual_all.at[k, n, c, flip_bits(z, off)]
            forwards.append(
                go(remote(slot, slot, fwd_sem.at[n, off - 1], partner))
            )
        gather[n] = forwards
        price_half[n] = nn(a_t[c], dual_all[k, n, c].reshape(half, chunk))

    def price_stage(k, n):
        for copy in gather[n]:
            copy.wait_recv()
        value = price_half[n] + nn(a_t[1 - c], dual_all[k, n, 1 - c].reshape(half, chunk))
        price_send[k, n, 0] = value.astype(BF16)
        price_go(k, n, 0)

    def price_go(k, n, turn):
        copies = []
        for h in range(2):
            bit = turn if h == 0 else turns - 1 - turn
            to = i + (1 - 2 * ((i // 2**bit) % 2)) * 2**bit
            at = slice(h * (units // 2), (h + 1) * (units // 2))
            copies.append(
                go(
                    remote(
                        price_send.at[k, n, turn, at],
                        price_recv.at[k, n, turn, at],
                        pr_sem.at[n, turn, h],
                        (to, j),
                    )
                )
            )
        pending[n] = copies

    def mix_stage(turn, k, n):
        for h in range(2):
            pending[n][h].wait_recv()
        value = price_send[k, n, turn - 1].astype(F32) + price_recv[k, n, turn - 1].astype(F32)
        price_send[k, n, turn] = value.astype(BF16)
        price_go(k, n, turn)

    bal_copies = []
    returns = {}
    writes = []

    def write(source, into, which, n):
        copy = pltpu.make_async_copy(source, into, in_sem.at[len(writes)])
        copy.start()
        writes.append(copy)

    def take_balance(k):
        for copy in bal_copies:
            copy.wait_recv()
        bal_copies.clear()
        balance = bal_recv[k, 0]
        for a in range(1, buses_n):
            balance = balance + bal_recv[k, a]
        for n in range(chunks):
            hold["lam"][n] = hold["lam"][n] + (KAPPA / total_units) * balance[:, cut(n)]

    def update_stage(k, n):
        if k == 0:
            for copy in state_shared[n]:
                copy.wait_recv()
        gen_0 = state_recv[n].reshape(width, chunk).astype(F32)
        stor_0 = hold["stor"][:, cut(n)]
        if k == 0:
            gen_now, stor_now = (gen_0, stor_0)
            gen_mid, stor_mid = (gen_0, stor_0)
        else:
            if n == 0:
                take_balance(0)
            gen_now, stor_now = (gen_keep[:, cut(n)], stor_keep[:, cut(n)])
            gen_mid = gen_now + THETA * (gen_now - gen_0)
            stor_mid = stor_now + THETA * (stor_now - stor_0)
        for copy in pending[n]:
            copy.wait_recv()
        price = price_send[k, n, turns - 1].astype(F32) + price_recv[k, n, turns - 1].astype(F32)
        lam = hold["lam"][n]
        gen_grad = 2.0 * slot_quad * gen_mid + slot_lin + lam + price[:width]
        gen_next = jnp.clip(gen_mid - TAU * gen_grad, 0.0, slot_max)
        stor_grad = 2.0 * hold["quad"] * stor_mid + lam + price[width:] + hold["back"][:, cut(n)]
        stor_next = jnp.clip(stor_mid - TAU * stor_grad, -hold["rate"], hold["rate"])
        gen_bar = 2.0 * gen_next - gen_now
        stor_bar = 2.0 * stor_next - stor_now
        bar_low = jnp.concatenate([gen_bar.astype(BF16), stor_bar.astype(BF16)], axis=0)

        def flow_half(w):
            value = nn(a_n[w], bar_low) - load_flow[w, :, cut(n)]
            flow_part[k, n, w] = value.astype(BF16).reshape(chips, share, chunk)

        flow_half(1 - c)
        pending[n] = go(
            remote(
                flow_part.at[k, n, 1 - c],
                pair_recv.at[k, n],
                pair_sem.at[n],
                partner,
            )
        )
        flow_half(c)
        bal_send[k, :, cut(n)] = (
            jnp.sum(gen_bar, axis=0, keepdims=True)
            + jnp.sum(stor_bar, axis=0, keepdims=True)
            - load_total[n]
        )
        bar_keep[:, cut(n)] = stor_bar
        if k == 0:
            gen_keep[:, cut(n)] = gen_next
            stor_keep[:, cut(n)] = stor_next
        else:
            gen_last[:, :, :, cut(n)] = gen_next.astype(BF16).reshape(lines_n, blocks, slots, chunk)
            returns[n] = []
            for off in range(1, buses_n):
                to = lax.rem(j + off, buses_n)
                source = lax.rem(j - off + buses_n, buses_n)
                returns[n].append(
                    go(
                        Guarded(
                            remote(
                                gen_last.at[to % lines_n, to // lines_n, :, cut(n)],
                                ret_all.at[n, i, j // lines_n],
                                ret_sem.at[n, off - 1],
                                (i, to),
                            ),
                            mine_now,
                            source % lines_n == i,
                        )
                    )
                )

            @pl.when(mine_now)
            def _():
                ret_all[n, i, j // lines_n] = gen_last[i, j // lines_n, :, cut(n)]

            stor_part[cut(n), :] = flipped(stor_next)
            write(stor_part.at[cut(n)], stor_out.at[cut(n)], 1, n)
        if n < chunks - 1:
            return
        bal_recv[k, j] = bal_send[k]
        for off in range(1, buses_n):
            bal_copies.append(
                go(
                    remote(
                        bal_send.at[k],
                        bal_recv.at[k, j],
                        par_sem.at[off - 1] if k == 0 else state_sem.at[0, off - 1],
                        (i, lax.rem(j + off, buses_n)),
                    )
                )
            )

    def pair_stage(k, n):
        pending[n].wait_recv()
        copies = []
        for off in masks:
            to = flip_bits(z, off)
            value = flow_part[k, n, c, to].astype(F32) + pair_recv[k, n, to].astype(F32)
            line_part[k, n, off] = value.astype(BF16)
            copies.append(
                go(
                    remote(
                        line_part.at[k, n, off],
                        line_recv.at[k, n, off],
                        line_sem.at[n, off - 1],
                        (i, to * 2 + c),
                    )
                )
            )
        pending[n] = copies
        if n == chunks - 1:
            charge = summed(bar_keep[...], hold["earlier"])
            shifted = hold["omega"] + SIGMA_STORE * charge
            high = hold["high"]
            omega = shifted - SIGMA_STORE * jnp.clip(shifted / SIGMA_STORE, -high, high)
            if k == 0:
                hold["omega"] = omega
                hold["back"] = summed(omega, hold["later"])
            else:
                omega_part[...] = flipped(omega)
                write(omega_part, omega_out, 3, 0)

    def dual_stage(k, n):
        flow = flow_part[k, n, c, z].astype(F32) + pair_recv[k, n, z].astype(F32)
        for off, copy in zip(masks, pending[n]):
            copy.wait_recv()
            flow = flow + line_recv[k, n, off].astype(F32)
        shifted = hold["mu"][n] + SIGMA_FLOW * flow
        limit = hold["limit"]
        mu = shifted - SIGMA_FLOW * jnp.clip(shifted / SIGMA_FLOW, -limit, limit)
        if k == 0:
            hold["mu"][n] = mu
            dual_all[1, n, c, z] = mu.astype(BF16)
            gather[n] = gather_start(1, n)
        else:
            mu_part[cut(n), :] = flipped(mu)
            write(mu_part.at[cut(n)], mu_out.at[cut(n)], 2, n)

    def return_stage(n):
        for copy in returns[n]:
            copy.wait_recv()
        returns[n] = []
        for off in range(1, lines_n):
            returns[n].append(
                go(
                    remote(
                        ret_all.at[n, i],
                        ret_all.at[n, i],
                        rag_sem.at[n, off - 1],
                        (lax.rem(i + off, lines_n), j),
                    )
                )
            )

    def result_stage(n):
        for copy in returns[n]:
            copy.wait_recv()
        gen_part[cut(n), :] = lax.dot_general(
            ret_all[n].reshape(width, chunk),
            back_place[...],
            (((0,), (0,)), ((), ())),
            preferred_element_type=F32,
        )
        write(gen_part.at[cut(n)], gen_out.at[cut(n)], 0, n)

    kinds = [("f", forward_stage), ("p", price_stage)]
    for turn in range(1, turns):
        kinds.append(("m", functools.partial(mix_stage, turn)))
    kinds += [("u", update_stage), ("a", pair_stage), ("d", dual_stage)]
    stages = [(kind, functools.partial(stage, k)) for k in range(2) for kind, stage in kinds]
    tail = [("r", return_stage), ("s", result_stage)]
    queue = [list(stages) for n in range(chunks)]
    ends = [list(tail) for n in range(chunks)]
    if chunks == 3 and turns == 2:
        order = " ".join(ORDER).split()
    else:
        order = ["l0"] + [kind + str(n) for kind, _ in stages + tail for n in range(chunks)]
    for entry in order:
        kind, n = (entry[0], int(entry[1:]))
        if kind == "l":
            stage = lambda n: late_setup()
        else:
            kind, stage = (ends if kind in "rs" else queue)[n].pop(0)
        stage(n)
        drain(DRAIN)
    take_balance(1)
    lam_part[...] = jnp.concatenate(hold["lam"], axis=1)
    write(lam_part, lam_out, 3, 1)
    for copy in writes:
        copy.wait()
    drain(0)


def finish(*refs):
    count = len(refs) // 2
    for source, result in zip(refs[:count], refs[count:]):
        result[...] = source[...].reshape(result.shape)


def shards(
    ptdf,
    load,
    ratings,
    line_index,
    gen_bus,
    gen_quad,
    gen_lin,
    gen_max,
    gen_start,
    stor_bus,
    stor_quad,
    stor_rate,
    stor_energy,
    stor_start,
    lam_start,
    mu_start,
    omega_start,
):
    lines_n = lax.axis_size("lines")
    buses_n = lax.axis_size("buses")
    rows, bus_count = load.shape
    line_count = ptdf.shape[0]
    gens = gen_bus.shape[0]
    stors = stor_bus.shape[0]
    share = line_count // buses_n
    chips = buses_n // 2
    slots = max(8, (gens + buses_n - 1) // buses_n)
    slots = (slots + 15) // 16 * 16
    width = buses_n * slots
    units = width + stors
    blocks = buses_n // lines_n
    turns = lines_n.bit_length() - 1
    half = line_count // 2
    chunk = 128 if rows % 128 == 0 else rows
    chunks = rows // chunk
    vmem = pl.BlockSpec(memory_space=pltpu.VMEM)
    hbm = pl.BlockSpec(memory_space=pl.ANY)
    dma = pltpu.SemaphoreType.DMA
    outs = pl.pallas_call(
        functools.partial(kernel, lines_n, buses_n, slots),
        out_shape=(
            jax.ShapeDtypeStruct((rows, gens), F32),
            jax.ShapeDtypeStruct((rows, stors), F32),
            jax.ShapeDtypeStruct((1, rows), F32),
            jax.ShapeDtypeStruct((rows, share), F32),
            jax.ShapeDtypeStruct((rows, stors), F32),
        ),
        in_specs=[hbm if n in (1, 2, 7, 12, 14, 15, 16) else vmem for n in range(17)],
        out_specs=(hbm,) * 5,
        scratch_shapes=[
            pltpu.VMEM((line_count, bus_count), BF16),
            pltpu.VMEM((rows, bus_count), F32),
            pltpu.VMEM((rows, bus_count), BF16),
            pltpu.VMEM((2, half, rows), F32),
            pltpu.VMEM((units, bus_count), BF16),
            pltpu.VMEM((4, width), F32),
            pltpu.VMEM((buses_n, 4, width), F32),
            pltpu.VMEM((width, buses_n * 4), F32),
            pltpu.VMEM((chunks, buses_n, slots, chunk), BF16),
            pltpu.VMEM((chunks, lines_n, blocks, slots, chunk), BF16),
            pltpu.VMEM((2, units, half), BF16),
            pltpu.VMEM((2, half, units), BF16),
            pltpu.VMEM((2, chunks, 2, chips, share, chunk), BF16),
            pltpu.VMEM((chunks, units, chunk), F32),
            pltpu.VMEM((2, chunks, turns, units, chunk), BF16),
            pltpu.VMEM((2, chunks, turns, units, chunk), BF16),
            pltpu.VMEM((width, rows), F32),
            pltpu.VMEM((stors, rows), F32),
            pltpu.VMEM((stors, rows), F32),
            pltpu.VMEM((lines_n, blocks, slots, rows), BF16),
            pltpu.VMEM((chunks, lines_n, blocks, slots, chunk), BF16),
            pltpu.VMEM((2, chunks, 2, chips, share, chunk), BF16),
            pltpu.VMEM((2, chunks, chips, share, chunk), BF16),
            pltpu.VMEM((2, chunks, chips, share, chunk), BF16),
            pltpu.VMEM((2, chunks, chips, share, chunk), BF16),
            pltpu.VMEM((2, 1, rows), F32),
            pltpu.VMEM((2, buses_n, 1, rows), F32),
            pltpu.VMEM((rows, gens), F32),
            pltpu.VMEM((rows, stors), F32),
            pltpu.VMEM((rows, stors), F32),
            pltpu.VMEM((rows, share), F32),
            pltpu.VMEM((ratings.shape[0] // 128, 128), F32),
            dma((max(7, 3 * chunks + 2),)),
            dma((POOL,)),
            dma((buses_n - 1,)),
            dma(((chunks + lines_n - 1) // lines_n, buses_n - 1)),
            dma((chunks, lines_n - 1)),
            dma((chunks, chips)),
            dma((chunks, chips - 1)),
            dma((chunks, turns, 2)),
            dma((chunks,)),
            dma((chunks, chips - 1)),
            dma((chunks, buses_n - 1)),
            dma((chunks, lines_n - 1)),
            pltpu.VMEM((width, gens), BF16),
            pltpu.VMEM((rows, gens), F32),
            pltpu.VMEM((rows, stors), F32),
            pltpu.VMEM((1, rows), F32),
            pltpu.VMEM((rows, share), F32),
            pltpu.VMEM((rows, stors), F32),
        ],
        compiler_params=pltpu.CompilerParams(
            collective_id=0, has_side_effects=True, vmem_limit_bytes=60 * 1024 * 1024
        ),
    )(
        gen_bus[None, :],
        mu_start,
        ratings.reshape(-1, 128),
        line_index.reshape(buses_n, share),
        gen_quad[None, :],
        gen_lin[None, :],
        gen_max[None, :],
        gen_start,
        stor_bus[None, :],
        stor_quad[None, :],
        stor_rate[None, :],
        stor_energy[None, :],
        stor_start,
        lam_start,
        omega_start,
        ptdf,
        load,
    )
    shapes = [x.shape for x in outs]
    shapes[2] = (rows,)
    return pl.pallas_call(
        finish,
        out_shape=tuple(jax.ShapeDtypeStruct(shape, F32) for shape in shapes),
        in_specs=[vmem] * 5,
        out_specs=(vmem,) * 5,
    )(*outs)


def solution(mesh):
    return jax.shard_map(
        shards,
        mesh=mesh,
        in_specs=(
            P("lines", "buses"),
            P(None, "buses"),
            P(),
            P("lines"),
            P("buses"),
            P("buses"),
            P("buses"),
            P("buses"),
            P(None, "buses"),
            P("buses"),
            P("buses"),
            P("buses"),
            P("buses"),
            P(None, "buses"),
            P(),
            P(None, ("lines", "buses")),
            P(None, "buses"),
        ),
        out_specs=(
            P(None, "buses"),
            P(None, "buses"),
            P(),
            P(None, ("lines", "buses")),
            P(None, "buses"),
        ),
        check_vma=False,
    )
```

```python
import functools
import jax
import jax.numpy as jnp
from jax import lax
from jax.experimental import pallas as pl
from jax.experimental.pallas import tpu as pltpu
from jax.sharding import PartitionSpec as P

HOURS = 24
TAU = 0.25
SIGMA_FLOW = 4.0
SIGMA_STORE = 0.25
KAPPA = 1.0
THETA = 0.5

F32 = jnp.float32
BF16 = jnp.bfloat16
MESH = pl.DeviceIdType.MESH
DRAIN = 12
POOL = 30
ORDER = (
    "f0 p0 l0 m0",
    "f1 p1 f2 p2",
    "m1 u0 m2 a0",
    "u1 a1 d0 u2",
    "a2 d1 f0 p0",
    "d2 f1 m0 p1",
    "f2 u0 p2 m1",
    "a0 m2 u1 a1",
    "u2 d0 a2 r0",
    "r1 d1 r2 s0",
    "s1 d2 s2",
)
HIGHEST = lax.Precision.HIGHEST


def nt(a, b, precision=None):
    return lax.dot_general(
        a, b, (((1,), (1,)), ((), ())), preferred_element_type=F32, precision=precision
    )


def nn(a, b, precision=None):
    return lax.dot_general(
        a, b, (((1,), (0,)), ((), ())), preferred_element_type=F32, precision=precision
    )


def iota(shape, dim):
    return lax.broadcasted_iota(jnp.int32, shape, dim)


def eye(n):
    return iota((n, n), 0) == iota((n, n), 1)


def summed(x, mask):
    high = x.astype(BF16)
    rest = x - high.astype(F32)
    mid = rest.astype(BF16)
    low = (rest - mid.astype(F32)).astype(BF16)
    return nn(high, mask) + (nn(mid, mask) + nn(low, mask))


def masked_sum(mask, x):
    high = x.astype(BF16)
    rest = x - high.astype(F32)
    mid = rest.astype(BF16)
    low = (rest - mid.astype(F32)).astype(BF16)
    mask = mask.astype(BF16)
    return nn(mask, high) + (nn(mask, mid) + nn(mask, low))


def flipped(x):
    if x.shape[0] % 128 == 0 and x.shape[1] % 128 == 0:
        return x.T
    return nt(eye(x.shape[1]).astype(F32), x, HIGHEST)


def to_column(row):
    n = row.shape[1]
    return jnp.sum(jnp.where(eye(n), row, 0.0), axis=1, keepdims=True)


def to_row(column):
    n = column.shape[0]
    return jnp.sum(jnp.where(eye(n), column, 0.0), axis=0, keepdims=True)


def remote_copy(src, dst, send_sem, recv_sem, target):
    return pltpu.make_async_remote_copy(
        src_ref=src,
        dst_ref=dst,
        send_sem=send_sem,
        recv_sem=recv_sem,
        device_id=target,
        device_id_type=MESH,
    )


class Sent:
    def __init__(self, copy, slot):
        self.copy = copy
        self.slot = slot

    def start(self):
        self.copy.start()

    def wait_send(self):
        self.copy.wait_send()

    def wait_recv(self):
        self.copy.wait_recv()


class Guarded:
    def __init__(self, copy, sends, receives):
        self.copy = copy
        self.slot = copy.slot
        self.sends = sends
        self.receives = receives

    def start(self):
        pl.when(self.sends)(lambda: self.copy.start())

    def wait_send(self):
        pl.when(self.sends)(lambda: self.copy.wait_send())

    def wait_recv(self):
        pl.when(self.receives)(lambda: self.copy.wait_recv())


def flip_bits(value, mask):
    bit = 1
    while bit <= mask:
        if mask // bit % 2:
            value = value + (1 - 2 * ((value // bit) % 2)) * bit
        bit *= 2
    return value


def kernel(
    lines_n,
    buses_n,
    slots,
    gen_bus,
    mu_in_hbm,
    ratings_hbm,
    line_index,
    gen_quad,
    gen_lin,
    gen_max,
    gen_start_hbm,
    stor_bus,
    stor_quad,
    stor_rate,
    stor_energy,
    stor_start_hbm,
    lam_in,
    omega_in_hbm,
    ptdf_hbm,
    load_hbm,
    gen_out,
    stor_out,
    lam_out,
    mu_out,
    omega_out,
    ptdf,
    load,
    load_low,
    load_flow,
    hits,
    par_send,
    par_all,
    par_turned,
    state_send,
    state_recv,
    a_t,
    a_n,
    dual_all,
    price_half,
    price_send,
    price_recv,
    gen_keep,
    stor_keep,
    bar_keep,
    gen_last,
    ret_all,
    flow_part,
    pair_recv,
    line_part,
    line_recv,
    bal_send,
    bal_recv,
    gen_start,
    stor_start,
    omega_in,
    mu_in,
    ratings,
    in_sem,
    send_sem,
    par_sem,
    state_sem,
    share_sem,
    ag_sem,
    fwd_sem,
    pr_sem,
    pair_sem,
    line_sem,
    ret_sem,
    rag_sem,
    back_place,
    gen_part,
    stor_part,
    lam_part,
    mu_part,
    omega_part,
):
    rows = load.shape[0]
    line_count, bus_count = ptdf.shape
    gens = gen_bus.shape[1]
    stors = stor_bus.shape[1]
    share = mu_in.shape[1]
    chips = buses_n // 2
    width = buses_n * slots
    units = width + stors
    half = line_count // 2
    blocks = buses_n // lines_n
    turns = price_send.shape[2]
    total_units = (gens + stors) * buses_n
    i = lax.axis_index("lines")
    j = lax.axis_index("buses")
    z = j // 2
    c = j % 2
    partner = (i, z * 2 + (1 - c))
    masks = list(range(1, chips))
    mine_now = j % lines_n == i
    chunk = dual_all.shape[-1]
    chunks = rows // chunk

    def cut(n):
        return slice(n * chunk, (n + 1) * chunk)

    load_copy = pltpu.make_async_copy(load_hbm, load, in_sem.at[0])
    ptdf_copy = pltpu.make_async_copy(ptdf_hbm, ptdf, in_sem.at[1])
    small_copies = [
        pltpu.make_async_copy(source, into, in_sem.at[2 + n])
        for n, (source, into) in enumerate(
            (
                (mu_in_hbm, mu_in),
                (gen_start_hbm, gen_start),
                (ratings_hbm, ratings),
                (stor_start_hbm, stor_start),
                (omega_in_hbm, omega_in),
            )
        )
    ]
    for copy in small_copies:
        copy.start()
    ptdf_copy.start()
    load_copy.start()

    barrier = pltpu.get_barrier_semaphore()
    for off in range(1, buses_n):
        pl.semaphore_signal(
            barrier, inc=1, device_id=(i, lax.rem(j + off, buses_n)), device_id_type=MESH
        )
    for off in range(1, lines_n):
        pl.semaphore_signal(
            barrier, inc=1, device_id=(lax.rem(i + off, lines_n), j), device_id_type=MESH
        )

    bus = gen_bus[...]
    target = bus // bus_count
    target_hit = iota((buses_n, gens), 0) == target
    upto = (iota((gens, gens), 0) <= iota((gens, gens), 1)).astype(BF16)
    count = nn(target_hit.astype(BF16), upto)
    rank = jnp.sum(jnp.where(target_hit, count, 0.0), axis=0, keepdims=True).astype(jnp.int32) - 1
    place = (iota((width, gens), 0) == target * slots + rank).astype(BF16)
    params = jnp.concatenate(
        [(bus - target * bus_count + 1).astype(F32), gen_quad[...], gen_lin[...], gen_max[...]], axis=0
    )
    high = params.astype(BF16)
    rest = params - high.astype(F32)
    mid = rest.astype(BF16)
    low = (rest - mid.astype(F32)).astype(BF16)
    par_send[...] = nt(high, place) + (nt(mid, place) + nt(low, place))
    par_all[j] = par_send[...]

    small_copies[0].wait()
    mu = flipped(mu_in[...])
    for n in range(chunks):
        dual_all[0, n, c, z] = mu[:, cut(n)].astype(BF16)
    small_copies[1].wait()
    state = nt(place, gen_start[...].astype(BF16)).astype(BF16)
    for n in range(chunks):
        state_send[n] = state[:, cut(n)].reshape(buses_n, slots, chunk)
    for n in range(chunks):

        @pl.when((j + n) % lines_n == i)
        def _(n=n):
            state_recv[n, j % lines_n, j // lines_n] = state_send[n, j]

    pl.semaphore_wait(barrier, buses_n + lines_n - 2)

    started = []
    stage_count = [0]

    holders = {}

    def remote(source, into, arrived, target):
        slot = min(range(POOL), key=lambda s: holders[s][0] if s in holders else -1)
        if slot in holders and holders[slot][1] in started:
            started.remove(holders[slot][1])
            holders[slot][1][1].wait_send()
        holders[slot] = (len(holders) and max(h[0] for h in holders.values()) + 1, None)
        return Sent(remote_copy(source, into, send_sem.at[slot], arrived, target), slot)

    def go(copy):
        copy.start()
        entry = (stage_count[0], copy)
        started.append(entry)
        holders[copy.slot] = (holders[copy.slot][0], entry)
        return copy

    def drain(age):
        stage_count[0] += 1
        while started and started[0][0] + age <= stage_count[0]:
            started.pop(0)[1].wait_send()

    par_copies = []
    for off in range(1, buses_n):
        to = (i, lax.rem(j + off, buses_n))
        par_copies.append(
            go(remote(par_send, par_all.at[j], par_sem.at[off - 1], to))
        )

    def gather_start(k, n):
        mine = dual_all.at[k, n, c, z]
        copies = []
        for off in masks:
            copies.append(
                go(
                    remote(
                        mine,
                        mine,
                        ag_sem.at[n, off],
                        (i, flip_bits(z, off) * 2 + c),
                    )
                )
            )
        copies.append(go(remote(mine, mine, ag_sem.at[n, 0], partner)))
        return copies

    state_copies = []
    for base in range(0, chunks, lines_n):
        for off in range(1, buses_n):
            to = lax.rem(j + off, buses_n)
            source = lax.rem(j - off + buses_n, buses_n)
            at = base + (i - j + buses_n) % lines_n
            held = jnp.minimum(at, chunks - 1)
            state_copies.append(
                go(
                    Guarded(
                        remote(
                            state_send.at[held, to],
                            state_recv.at[held, j % lines_n, j // lines_n],
                            state_sem.at[base // lines_n, off - 1],
                            (i, to),
                        ),
                        at < chunks,
                        base + (i - source + buses_n) % lines_n < chunks,
                    )
                )
            )
    gather = [gather_start(0, 0)]

    stor_column = to_column(stor_bus[...].astype(F32)).astype(jnp.int32)
    hits[width:, :] = (iota((stors, bus_count), 1) == stor_column).astype(BF16)
    for copy in small_copies[2:]:
        copy.wait()
    load_copy.wait()
    load_value = load[...]
    load_total = jnp.sum(load_value, axis=1, keepdims=True)
    load_total = [to_row(load_total[cut(n), :]) for n in range(chunks)]
    load_low[...] = load_value.astype(BF16)
    ptdf_copy.wait()
    wide = max(512, 2 * share) if line_count % 512 == 0 else max(256, 2 * share)
    group = wide // (2 * share)
    step = wide // 2

    def lines_of(t, w):
        block = ptdf[pl.ds(pl.multiple_of(t * wide, wide), wide), :]
        return block.reshape(group, 2, share, bus_count)[:, w].reshape(step, bus_count)

    def load_step(t, carry):
        at = pl.multiple_of(t * step, step)
        for w in range(2):
            load_flow[w, pl.ds(at, step), :] = nt(lines_of(t, w), load_low[...])
        return carry

    lax.fori_loop(0, line_count // wide, load_step, 0)
    for n in range(1, min(2, chunks)):
        gather.append(gather_start(0, n))
    hold = {"mu": [mu[:, cut(n)] for n in range(chunks)]}
    wanted = jnp.sum(
        jnp.where(iota((buses_n, share), 0) == j, line_index[...].astype(F32), 0.0),
        axis=0,
        keepdims=True,
    )
    wanted = to_column(wanted).astype(jnp.int32)
    lanes = ratings.shape[1]
    high_hit = (iota((share, ratings.shape[0]), 1) == wanted // lanes).astype(F32)
    rated = masked_sum(high_hit, ratings[...])
    hold["limit"] = jnp.sum(
        jnp.where(iota((share, lanes), 1) == wanted % lanes, rated, 0.0), axis=1, keepdims=True
    )
    hold["omega"] = flipped(omega_in[...])
    row_id, col_id = (iota((rows, rows), 0), iota((rows, rows), 1))
    same = row_id // HOURS == col_id // HOURS
    hold["later"] = jnp.where(same & (row_id >= col_id), 1.0, 0.0).astype(BF16)
    hold["earlier"] = jnp.where(same & (row_id <= col_id), 1.0, 0.0).astype(BF16)
    hold["back"] = summed(hold["omega"], hold["later"])
    hold["stor"] = flipped(stor_start[...])
    lam_row = lam_in[...].reshape(1, rows)
    hold["lam"] = [lam_row[:, cut(n)] for n in range(chunks)]
    hold["quad"] = to_column(stor_quad[...])
    hold["rate"] = to_column(stor_rate[...])
    hour = iota((1, rows), 1) % HOURS
    hold["high"] = jnp.where(hour == HOURS - 1, 0.0, to_column(0.5 * stor_energy[...]))

    for copy in par_copies:
        copy.wait_recv()
    every = jnp.concatenate([par_all[a] for a in range(buses_n)], axis=0)
    par_turned[...] = every.T
    mine = par_turned[pl.ds(pl.multiple_of(j * slots, slots), slots), :]

    owners = [q * lines_n + g for g in range(lines_n) for q in range(blocks)]

    def slot_column(p):
        return jnp.concatenate([mine[:, a * 4 + p : a * 4 + p + 1] for a in owners], axis=0)

    slot_bus = slot_column(0).astype(jnp.int32) - 1
    slot_quad, slot_lin, slot_max = (slot_column(1), slot_column(2), slot_column(3))
    hits[:width, :] = (iota((width, bus_count), 1) == slot_bus).astype(BF16)

    def turn_step(t, carry):
        at = pl.multiple_of(t * step, step)
        for w in range(2):
            a_t[w, :, pl.ds(at, step)] = nt(hits[...], lines_of(t, w)).astype(BF16)
        return carry

    state_shared = []

    def share_state():
        for copy in state_copies:
            copy.wait_recv()
        for n in range(chunks):
            state_shared.append([])
            held = state_recv.at[n, (i - n + chunks * lines_n) % lines_n]
            for off in range(1, lines_n):
                to = (lax.rem(i + off, lines_n), j)
                state_shared[n].append(go(remote(held, held, share_sem.at[n, off - 1], to)))

    share_state()
    for n in range(2, chunks):
        gather.append(gather_start(0, n))
    lax.fori_loop(0, line_count // wide, turn_step, 0)

    def late_setup():
        def flow_step(t, carry):
            at = pl.multiple_of(t * step, step)
            for w in range(2):
                a_n[w, pl.ds(at, step), :] = nt(lines_of(t, w), hits[...]).astype(BF16)
            return carry

        lax.fori_loop(0, line_count // wide, flow_step, 0)
        spot = ((target % lines_n) * blocks + target // lines_n) * slots + rank
        back_place[...] = (iota((width, gens), 0) == spot).astype(BF16)

    pending = {}

    def forward_stage(k, n):
        copies = gather[n]
        forwards = [copies[-1]]
        for off, copy in zip(masks, copies):
            copy.wait_recv()
            slot = dual_all.at[k, n, c, flip_bits(z, off)]
            forwards.append(
                go(remote(slot, slot, fwd_sem.at[n, off - 1], partner))
            )
        gather[n] = forwards
        price_half[n] = nn(a_t[c], dual_all[k, n, c].reshape(half, chunk))

    def price_stage(k, n):
        for copy in gather[n]:
            copy.wait_recv()
        value = price_half[n] + nn(a_t[1 - c], dual_all[k, n, 1 - c].reshape(half, chunk))
        price_send[k, n, 0] = value.astype(BF16)
        price_go(k, n, 0)

    def price_go(k, n, turn):
        copies = []
        for h in range(2):
            bit = turn if h == 0 else turns - 1 - turn
            to = i + (1 - 2 * ((i // 2**bit) % 2)) * 2**bit
            at = slice(h * (units // 2), (h + 1) * (units // 2))
            copies.append(
                go(
                    remote(
                        price_send.at[k, n, turn, at],
                        price_recv.at[k, n, turn, at],
                        pr_sem.at[n, turn, h],
                        (to, j),
                    )
                )
            )
        pending[n] = copies

    def mix_stage(turn, k, n):
        for h in range(2):
            pending[n][h].wait_recv()
        value = price_send[k, n, turn - 1].astype(F32) + price_recv[k, n, turn - 1].astype(F32)
        price_send[k, n, turn] = value.astype(BF16)
        price_go(k, n, turn)

    bal_copies = []
    returns = {}
    writes = []

    def write(source, into, which, n):
        copy = pltpu.make_async_copy(source, into, in_sem.at[len(writes)])
        copy.start()
        writes.append(copy)

    def take_balance(k):
        for copy in bal_copies:
            copy.wait_recv()
        bal_copies.clear()
        balance = bal_recv[k, 0]
        for a in range(1, buses_n):
            balance = balance + bal_recv[k, a]
        for n in range(chunks):
            hold["lam"][n] = hold["lam"][n] + (KAPPA / total_units) * balance[:, cut(n)]

    def update_stage(k, n):
        if k == 0:
            for copy in state_shared[n]:
                copy.wait_recv()
        gen_0 = state_recv[n].reshape(width, chunk).astype(F32)
        stor_0 = hold["stor"][:, cut(n)]
        if k == 0:
            gen_now, stor_now = (gen_0, stor_0)
            gen_mid, stor_mid = (gen_0, stor_0)
        else:
            if n == 0:
                take_balance(0)
            gen_now, stor_now = (gen_keep[:, cut(n)], stor_keep[:, cut(n)])
            gen_mid = gen_now + THETA * (gen_now - gen_0)
            stor_mid = stor_now + THETA * (stor_now - stor_0)
        for copy in pending[n]:
            copy.wait_recv()
        price = price_send[k, n, turns - 1].astype(F32) + price_recv[k, n, turns - 1].astype(F32)
        lam = hold["lam"][n]
        gen_grad = 2.0 * slot_quad * gen_mid + slot_lin + lam + price[:width]
        gen_next = jnp.clip(gen_mid - TAU * gen_grad, 0.0, slot_max)
        stor_grad = 2.0 * hold["quad"] * stor_mid + lam + price[width:] + hold["back"][:, cut(n)]
        stor_next = jnp.clip(stor_mid - TAU * stor_grad, -hold["rate"], hold["rate"])
        gen_bar = 2.0 * gen_next - gen_now
        stor_bar = 2.0 * stor_next - stor_now
        bar_low = jnp.concatenate([gen_bar.astype(BF16), stor_bar.astype(BF16)], axis=0)

        def flow_half(w):
            value = nn(a_n[w], bar_low) - load_flow[w, :, cut(n)]
            flow_part[k, n, w] = value.astype(BF16).reshape(chips, share, chunk)

        flow_half(1 - c)
        pending[n] = go(
            remote(
                flow_part.at[k, n, 1 - c],
                pair_recv.at[k, n],
                pair_sem.at[n],
                partner,
            )
        )
        flow_half(c)
        bal_send[k, :, cut(n)] = (
            jnp.sum(gen_bar, axis=0, keepdims=True)
            + jnp.sum(stor_bar, axis=0, keepdims=True)
            - load_total[n]
        )
        bar_keep[:, cut(n)] = stor_bar
        if k == 0:
            gen_keep[:, cut(n)] = gen_next
            stor_keep[:, cut(n)] = stor_next
        else:
            gen_last[:, :, :, cut(n)] = gen_next.astype(BF16).reshape(lines_n, blocks, slots, chunk)
            returns[n] = []
            for off in range(1, buses_n):
                to = lax.rem(j + off, buses_n)
                source = lax.rem(j - off + buses_n, buses_n)
                returns[n].append(
                    go(
                        Guarded(
                            remote(
                                gen_last.at[to % lines_n, to // lines_n, :, cut(n)],
                                ret_all.at[n, i, j // lines_n],
                                ret_sem.at[n, off - 1],
                                (i, to),
                            ),
                            mine_now,
                            source % lines_n == i,
                        )
                    )
                )

            @pl.when(mine_now)
            def _():
                ret_all[n, i, j // lines_n] = gen_last[i, j // lines_n, :, cut(n)]

            stor_part[cut(n), :] = flipped(stor_next)
            write(stor_part.at[cut(n)], stor_out.at[cut(n)], 1, n)
        if n < chunks - 1:
            return
        bal_recv[k, j] = bal_send[k]
        for off in range(1, buses_n):
            bal_copies.append(
                go(
                    remote(
                        bal_send.at[k],
                        bal_recv.at[k, j],
                        par_sem.at[off - 1] if k == 0 else state_sem.at[0, off - 1],
                        (i, lax.rem(j + off, buses_n)),
                    )
                )
            )

    def pair_stage(k, n):
        pending[n].wait_recv()
        copies = []
        for off in masks:
            to = flip_bits(z, off)
            value = flow_part[k, n, c, to].astype(F32) + pair_recv[k, n, to].astype(F32)
            line_part[k, n, off] = value.astype(BF16)
            copies.append(
                go(
                    remote(
                        line_part.at[k, n, off],
                        line_recv.at[k, n, off],
                        line_sem.at[n, off - 1],
                        (i, to * 2 + c),
                    )
                )
            )
        pending[n] = copies
        if n == chunks - 1:
            charge = summed(bar_keep[...], hold["earlier"])
            shifted = hold["omega"] + SIGMA_STORE * charge
            high = hold["high"]
            omega = shifted - SIGMA_STORE * jnp.clip(shifted / SIGMA_STORE, -high, high)
            if k == 0:
                hold["omega"] = omega
                hold["back"] = summed(omega, hold["later"])
            else:
                omega_part[...] = flipped(omega)
                write(omega_part, omega_out, 3, 0)

    def dual_stage(k, n):
        flow = flow_part[k, n, c, z].astype(F32) + pair_recv[k, n, z].astype(F32)
        for off, copy in zip(masks, pending[n]):
            copy.wait_recv()
            flow = flow + line_recv[k, n, off].astype(F32)
        shifted = hold["mu"][n] + SIGMA_FLOW * flow
        limit = hold["limit"]
        mu = shifted - SIGMA_FLOW * jnp.clip(shifted / SIGMA_FLOW, -limit, limit)
        if k == 0:
            hold["mu"][n] = mu
            dual_all[1, n, c, z] = mu.astype(BF16)
            gather[n] = gather_start(1, n)
        else:
            mu_part[cut(n), :] = flipped(mu)
            write(mu_part.at[cut(n)], mu_out.at[cut(n)], 2, n)

    def return_stage(n):
        for copy in returns[n]:
            copy.wait_recv()
        returns[n] = []
        for off in range(1, lines_n):
            returns[n].append(
                go(
                    remote(
                        ret_all.at[n, i],
                        ret_all.at[n, i],
                        rag_sem.at[n, off - 1],
                        (lax.rem(i + off, lines_n), j),
                    )
                )
            )

    def result_stage(n):
        for copy in returns[n]:
            copy.wait_recv()
        gen_part[cut(n), :] = lax.dot_general(
            ret_all[n].reshape(width, chunk),
            back_place[...],
            (((0,), (0,)), ((), ())),
            preferred_element_type=F32,
        )
        write(gen_part.at[cut(n)], gen_out.at[cut(n)], 0, n)

    kinds = [("f", forward_stage), ("p", price_stage)]
    for turn in range(1, turns):
        kinds.append(("m", functools.partial(mix_stage, turn)))
    kinds += [("u", update_stage), ("a", pair_stage), ("d", dual_stage)]
    stages = [(kind, functools.partial(stage, k)) for k in range(2) for kind, stage in kinds]
    tail = [("r", return_stage), ("s", result_stage)]
    queue = [list(stages) for n in range(chunks)]
    ends = [list(tail) for n in range(chunks)]
    if chunks == 3 and turns == 2:
        order = " ".join(ORDER).split()
    else:
        order = ["l0"] + [kind + str(n) for kind, _ in stages + tail for n in range(chunks)]
    for entry in order:
        kind, n = (entry[0], int(entry[1:]))
        if kind == "l":
            stage = lambda n: late_setup()
        else:
            kind, stage = (ends if kind in "rs" else queue)[n].pop(0)
        stage(n)
        drain(DRAIN)
    take_balance(1)
    lam_part[...] = jnp.concatenate(hold["lam"], axis=1)
    write(lam_part, lam_out, 3, 1)
    for copy in writes:
        copy.wait()
    drain(0)


def finish(*refs):
    count = len(refs) // 2
    for source, result in zip(refs[:count], refs[count:]):
        result[...] = source[...].reshape(result.shape)


def shards(
    ptdf,
    load,
    ratings,
    line_index,
    gen_bus,
    gen_quad,
    gen_lin,
    gen_max,
    gen_start,
    stor_bus,
    stor_quad,
    stor_rate,
    stor_energy,
    stor_start,
    lam_start,
    mu_start,
    omega_start,
):
    lines_n = lax.axis_size("lines")
    buses_n = lax.axis_size("buses")
    rows, bus_count = load.shape
    line_count = ptdf.shape[0]
    gens = gen_bus.shape[0]
    stors = stor_bus.shape[0]
    share = line_count // buses_n
    chips = buses_n // 2
    slots = max(8, (gens + buses_n - 1) // buses_n)
    slots = (slots + 15) // 16 * 16
    width = buses_n * slots
    units = width + stors
    blocks = buses_n // lines_n
    turns = lines_n.bit_length() - 1
    half = line_count // 2
    chunk = 128 if rows % 128 == 0 else rows
    chunks = rows // chunk
    vmem = pl.BlockSpec(memory_space=pltpu.VMEM)
    hbm = pl.BlockSpec(memory_space=pl.ANY)
    dma = pltpu.SemaphoreType.DMA
    outs = pl.pallas_call(
        functools.partial(kernel, lines_n, buses_n, slots),
        out_shape=(
            jax.ShapeDtypeStruct((rows, gens), F32),
            jax.ShapeDtypeStruct((rows, stors), F32),
            jax.ShapeDtypeStruct((1, rows), F32),
            jax.ShapeDtypeStruct((rows, share), F32),
            jax.ShapeDtypeStruct((rows, stors), F32),
        ),
        in_specs=[hbm if n in (1, 2, 7, 12, 14, 15, 16) else vmem for n in range(17)],
        out_specs=(hbm,) * 5,
        scratch_shapes=[
            pltpu.VMEM((line_count, bus_count), BF16),
            pltpu.VMEM((rows, bus_count), F32),
            pltpu.VMEM((rows, bus_count), BF16),
            pltpu.VMEM((2, half, rows), F32),
            pltpu.VMEM((units, bus_count), BF16),
            pltpu.VMEM((4, width), F32),
            pltpu.VMEM((buses_n, 4, width), F32),
            pltpu.VMEM((width, buses_n * 4), F32),
            pltpu.VMEM((chunks, buses_n, slots, chunk), BF16),
            pltpu.VMEM((chunks, lines_n, blocks, slots, chunk), BF16),
            pltpu.VMEM((2, units, half), BF16),
            pltpu.VMEM((2, half, units), BF16),
            pltpu.VMEM((2, chunks, 2, chips, share, chunk), BF16),
            pltpu.VMEM((chunks, units, chunk), F32),
            pltpu.VMEM((2, chunks, turns, units, chunk), BF16),
            pltpu.VMEM((2, chunks, turns, units, chunk), BF16),
            pltpu.VMEM((width, rows), F32),
            pltpu.VMEM((stors, rows), F32),
            pltpu.VMEM((stors, rows), F32),
            pltpu.VMEM((lines_n, blocks, slots, rows), BF16),
            pltpu.VMEM((chunks, lines_n, blocks, slots, chunk), BF16),
            pltpu.VMEM((2, chunks, 2, chips, share, chunk), BF16),
            pltpu.VMEM((2, chunks, chips, share, chunk), BF16),
            pltpu.VMEM((2, chunks, chips, share, chunk), BF16),
            pltpu.VMEM((2, chunks, chips, share, chunk), BF16),
            pltpu.VMEM((2, 1, rows), F32),
            pltpu.VMEM((2, buses_n, 1, rows), F32),
            pltpu.VMEM((rows, gens), F32),
            pltpu.VMEM((rows, stors), F32),
            pltpu.VMEM((rows, stors), F32),
            pltpu.VMEM((rows, share), F32),
            pltpu.VMEM((ratings.shape[0] // 128, 128), F32),
            dma((max(7, 3 * chunks + 2),)),
            dma((POOL,)),
            dma((buses_n - 1,)),
            dma(((chunks + lines_n - 1) // lines_n, buses_n - 1)),
            dma((chunks, lines_n - 1)),
            dma((chunks, chips)),
            dma((chunks, chips - 1)),
            dma((chunks, turns, 2)),
            dma((chunks,)),
            dma((chunks, chips - 1)),
            dma((chunks, buses_n - 1)),
            dma((chunks, lines_n - 1)),
            pltpu.VMEM((width, gens), BF16),
            pltpu.VMEM((rows, gens), F32),
            pltpu.VMEM((rows, stors), F32),
            pltpu.VMEM((1, rows), F32),
            pltpu.VMEM((rows, share), F32),
            pltpu.VMEM((rows, stors), F32),
        ],
        compiler_params=pltpu.CompilerParams(
            collective_id=0, has_side_effects=True, vmem_limit_bytes=60 * 1024 * 1024
        ),
    )(
        gen_bus[None, :],
        mu_start,
        ratings.reshape(-1, 128),
        line_index.reshape(buses_n, share),
        gen_quad[None, :],
        gen_lin[None, :],
        gen_max[None, :],
        gen_start,
        stor_bus[None, :],
        stor_quad[None, :],
        stor_rate[None, :],
        stor_energy[None, :],
        stor_start,
        lam_start,
        omega_start,
        ptdf,
        load,
    )
    shapes = [x.shape for x in outs]
    shapes[2] = (rows,)
    return pl.pallas_call(
        finish,
        out_shape=tuple(jax.ShapeDtypeStruct(shape, F32) for shape in shapes),
        in_specs=[vmem] * 5,
        out_specs=(vmem,) * 5,
    )(*outs)


def solution(mesh):
    return jax.shard_map(
        shards,
        mesh=mesh,
        in_specs=(
            P("lines", "buses"),
            P(None, "buses"),
            P(),
            P("lines"),
            P("buses"),
            P("buses"),
            P("buses"),
            P("buses"),
            P(None, "buses"),
            P("buses"),
            P("buses"),
            P("buses"),
            P("buses"),
            P(None, "buses"),
            P(),
            P(None, ("lines", "buses")),
            P(None, "buses"),
        ),
        out_specs=(
            P(None, "buses"),
            P(None, "buses"),
            P(),
            P(None, ("lines", "buses")),
            P(None, "buses"),
        ),
        check_vma=False,
    )
```
